32 devices in a mesh: slab: 8 (over z, x), cable: 4 (over y, core).
Axes of the slice: x: 2, y: 2, z: 4, core: 2. Of those that a mesh axis runs over, the one named last changes fastest.
Arguments:
- electric: float32 [3, 256, 128, 256], P(None, ('slab', 'cable')), may hold values from -6 to 6
- magnetic: float32 [3, 256, 128, 256], P(None, ('slab', 'cable')), may hold values from -6 to 6
- conductivity: float32 [256, 128, 256], P(('slab', 'cable')), may hold values from 0.02 to 0.8
- voltage: float32 [32, 32, 4096], P(None, None, ('slab', 'cable')), may hold values from -6 to 6
- current: float32 [32, 32, 4096], P(None, None, ('slab', 'cable')), may hold values from -6 to 6
- inverse_inductance: float32 [32, 32, 4096], P(None, None, ('slab', 'cable')), as said below
- inverse_capacitance: float32 [32, 32, 4096], P(None, None, ('slab', 'cable')), as said below
- tangent: float32 [3, 32, 4096], P(None, ('slab', 'cable')), may hold values from -4 to 4
- sample_cell: int32 [32, 4096], P(('slab', 'cable')), may hold values from 0 to 1023
- tube_length: int32 [4096], P(('slab', 'cable')), may hold values from 8 to 32
- junction_link: int32 [4096], P(('slab', 'cable')), may hold values from 0 to 127, as said below
Outputs:
- electric_new: float32 [3, 256, 128, 256], P(None, ('slab', 'cable'))
- magnetic_new: float32 [3, 256, 128, 256], P(None, ('slab', 'cable'))
- voltage_new: float32 [32, 32, 4096], P(None, None, ('slab', 'cable'))
- current_new: float32 [32, 32, 4096], P(None, None, ('slab', 'cable'))
The draws below stay inside these ranges and needn't reach their ends.
Inputs may be any that keep to these rules, and one draw needn't show every extreme that they name: `junction_link`: every aligned block of 128 entries holds each of its values once. `inverse_inductance`: symmetric, with off-diagonal entries summing to about as much as the diagonal. `inverse_capacitance`: symmetric, with off-diagonal entries summing to about as much as the diagonal.
All inputs are finite; a program needn't handle non-finite values.
Results may differ from the reference program's by a relative error of at most 0.0001.
Values sent between devices are 32-bit elements; how exact they have to be, the bound alone decides.
A program may use at most 128 MiB of HBM per device.

```python
import math
import jax
import jax.numpy as jnp
from jax import lax

COND = 32
SUB = 3
SEG_DEV = 1
CX = 8
NY = 128
NZ = 256
TUBE_DEV = 128
NX = 256
SEG = 32
TUBES = 4096
N_CABLE = 4


def matrix_block(subkey):
    first, second = jax.random.split(subkey)
    diagonal = jax.random.uniform(first, (COND, TUBES), jnp.float32, 0.3, 0.6)
    spread = 0.025
    coupling = jax.random.normal(second, (COND, COND, TUBES), jnp.float32) * spread
    coupling = 0.5 * (coupling + jnp.transpose(coupling, (1, 0, 2)))
    identity = jnp.eye(COND, dtype=jnp.float32)[:, :, None]
    return coupling * (1.0 - identity) + identity * diagonal[None]


def draw_inverse_inductance(key, part):
    return matrix_block(jax.random.fold_in(key, 11))


def draw_inverse_capacitance(key, part):
    return matrix_block(jax.random.fold_in(key, 23))


def draw_tube_length(key, part):
    values = jax.random.randint(jax.random.fold_in(key, 5), (TUBES,), SEG // 4, SEG + 1).astype(jnp.int32)
    return values.at[0].set(SEG).at[1].set(SEG // 4)


def one_block(subkey):
    return jax.random.permutation(subkey, TUBE_DEV)


def draw_junction_link(key, part):
    subkeys = jax.random.split(jax.random.fold_in(key, 7), TUBES // TUBE_DEV)
    return jax.vmap(one_block)(subkeys).reshape(TUBES).astype(jnp.int32)


def with_ends(values, own_key, smallest, largest):
    longest = values.shape.index(max(values.shape))
    spots = []
    for shift in (0, 1):
        where = [jax.random.randint(jax.random.fold_in(own_key, axis), (), 0, length) for axis, length in enumerate(values.shape)]
        where[longest] = (where[longest] + shift) % values.shape[longest]
        spots.append(tuple(where))
    return values.at[spots[0]].set(smallest).at[spots[1]].set(largest)


def steps_of(rng, dims, cuts, low, top_value):
    def one(dim, shards_of):
        heights = jax.random.uniform(jax.random.fold_in(jax.random.fold_in(rng, 6), dim), (shards_of,), jnp.float32, low / len(cuts), top_value / len(cuts))
        return jnp.repeat(jnp.exp(heights), dims[dim] // shards_of).reshape((-1,) + (1,) * (len(dims) - dim - 1))

    level = one(*cuts[0])
    for cut in cuts[1:]:
        level = level * one(*cut)
    return level


def scatter_about(own_key, shape, deviation, most, pieces=(), held_as=jnp.bfloat16):
    array = jax.random.normal(own_key, shape, jnp.float32) * deviation
    if len(pieces) > 0:
        array = steps_of(own_key, shape, pieces, -0.22, 0.18) * array
    return jnp.clip(array, min=-most, max=most).astype(held_as)


def setup_inputs(seed: int = 0) -> dict:
    key_list = jax.random.split(jax.random.key(seed), 12)
    return {
        "electric": scatter_about(key_list[0], (3, NX, NY, NZ), 1.0, 6.0, ((1, 32),), jnp.float32),
        "magnetic": scatter_about(key_list[1], (3, NX, NY, NZ), 1.0, 6.0, ((1, 32),), jnp.float32),
        "conductivity": jnp.clip(jnp.exp(math.log(0.8) - 3.6888795 * jax.random.uniform(key_list[2], (NX, NY, NZ), jnp.float32) ** steps_of(key_list[2], (NX, NY, NZ), ((0, 32),), -0.2, 0.2)), 0.02, 0.8),
        "voltage": scatter_about(key_list[3], (COND, SEG, TUBES), 1.0, 6.0, ((2, 32),), jnp.float32),
        "current": scatter_about(key_list[4], (COND, SEG, TUBES), 1.0, 6.0, ((2, 32),), jnp.float32),
        "inverse_inductance": draw_inverse_inductance(jax.random.fold_in(key_list[11], 71), 0),
        "inverse_capacitance": draw_inverse_capacitance(jax.random.fold_in(key_list[11], 71), 0),
        "tangent": scatter_about(key_list[7], (3, SEG, TUBES), 1.0, 4.0, ((1, 32),), jnp.float32),
        "sample_cell": with_ends(jax.random.randint(key_list[8], (SEG, TUBES), 0, CX * NY), jax.random.fold_in(key_list[8], 1), 0, (CX * NY) - 1).astype(jnp.int32),
        "tube_length": draw_tube_length(jax.random.fold_in(key_list[11], 71), 0),
        "junction_link": draw_junction_link(jax.random.fold_in(key_list[11], 71), 0),
    }


courant = 0.5
highest = lax.Precision.HIGHEST


def forward_diff(quantity, along):
    extent = quantity.shape[along]
    shifted = jnp.concatenate([lax.slice_in_dim(quantity, 1, extent, axis=along), jnp.zeros_like(lax.slice_in_dim(quantity, 0, 1, axis=along))], axis=along)
    return shifted - quantity


def backward_diff(quantity, along):
    extent = quantity.shape[along]
    shifted = jnp.concatenate([jnp.zeros_like(lax.slice_in_dim(quantity, 0, 1, axis=along)), lax.slice_in_dim(quantity, 0, extent - 1, axis=along)], axis=along)
    return quantity - shifted


def reference(electric, magnetic, conductivity, voltage, current, inverse_inductance, inverse_capacitance, tangent, sample_cell, tube_length, junction_link):
    keep_factor = (1.0 - conductivity) / (1.0 + conductivity)
    curl_factor = courant / (1.0 + conductivity)
    magnetic_new = magnetic - courant * jnp.stack([
        forward_diff(electric[2], 1) - forward_diff(electric[1], 2),
        forward_diff(electric[0], 2) - forward_diff(electric[2], 0),
        forward_diff(electric[1], 0) - forward_diff(electric[0], 1)])
    segment_ids = jnp.arange(SEG, dtype=jnp.int32)
    tube_ids = jnp.arange(TUBES, dtype=jnp.int32)
    global_cell = (((segment_ids // SEG_DEV) * (CX * NY * NZ)).astype(jnp.int32)[:, None] + sample_cell * NZ + (tube_ids % NZ)[None, :]).astype(jnp.int32)
    flat_field = electric.reshape(3, -1)
    drive_field = tangent[0] * flat_field[0][global_cell] + tangent[1] * flat_field[1][global_cell] + tangent[2] * flat_field[2][global_cell]
    live = (segment_ids[:, None] < tube_length[None, :]).astype(jnp.float32)
    last_pick = (segment_ids[:, None] == (tube_length - 1)[None, :]).astype(jnp.float32)
    owner = jnp.arange(TUBES, dtype=jnp.int32) // TUBE_DEV
    feeder_owner = owner // N_CABLE * N_CABLE + (owner % N_CABLE + N_CABLE - 1) % N_CABLE
    feeder_tube = (feeder_owner * TUBE_DEV + junction_link).astype(jnp.int32)
    volts = voltage
    amps = current
    for substep in range(SUB):
        volts_next = jnp.concatenate([volts[:, 1:], jnp.zeros_like(volts[:, :1])], axis=1)
        push = volts_next - volts - drive_field[None]
        amps = live[None] * (amps - jnp.einsum('cdt,dst->cst', inverse_inductance, push, precision=highest))
        tube_end = jnp.sum(amps * last_pick[None], axis=1)
        inflow = tube_end[:, feeder_tube]
        amps_prev = jnp.concatenate([inflow[:, None], amps[:, :-1]], axis=1)
        volts = live[None] * (volts - jnp.einsum('cdt,dst->cst', inverse_capacitance, amps - amps_prev, precision=highest))
    induced = jnp.mean(amps, axis=0)
    flat_index = global_cell.reshape(-1)
    deposit = jnp.stack([jax.ops.segment_sum((tangent[component] * induced).reshape(-1), flat_index, num_segments=NX * NY * NZ) for component in range(3)]).reshape(electric.shape)
    curl_h = jnp.stack([
        backward_diff(magnetic_new[2], 1) - backward_diff(magnetic_new[1], 2),
        backward_diff(magnetic_new[0], 2) - backward_diff(magnetic_new[2], 0),
        backward_diff(magnetic_new[1], 0) - backward_diff(magnetic_new[0], 1)])
    electric_new = keep_factor[None] * electric + curl_factor[None] * (curl_h - deposit)
    return electric_new, magnetic_new, volts, amps
```

```python
import functools

import jax
import jax.numpy as jnp
from jax import lax
from jax.experimental import pallas as pl
from jax.experimental.pallas import tpu as pltpu
from jax.sharding import PartitionSpec as P

COURANT = 0.5
LANES = 128
SUBLANES = 8
AXES = ("slab", "cable")


def passed_along(x, axis, by):
    peers = lax.axis_size(axis)
    pairs = [(i, i + by) for i in range(peers) if 0 <= i + by < peers]
    return lax.ppermute(x, axis, pairs)


def passed_round(value, axis, steps):
    count = lax.axis_size(axis)
    pairs = [(source, (source + steps) % count) for source in range(count)]
    return lax.ppermute(value, axis, pairs)


def params(*semantics):
    if semantics:
        return pltpu.CompilerParams(dimension_semantics=semantics)
    return pltpu.CompilerParams()


def whole_block(shape):
    rank = len(shape)
    return pl.BlockSpec(shape, lambda i: (0,) * rank)


def gather_kernel(cell_ref, tangent_ref, field_ref, drive_ref, picked_ref):
    step = pl.program_id(0)
    block_rows, nz = field_ref.shape[1], field_ref.shape[2]
    halves = nz // LANES
    trays = cell_ref.shape[0] // halves
    groups = trays // SUBLANES
    chunks = block_rows // SUBLANES

    @pl.when(step == 0)
    def _():
        picked_ref[...] = jnp.zeros_like(picked_ref)

    for half in range(halves):
        for group in range(groups):
            start = group * SUBLANES * halves + half
            cells = cell_ref[pl.ds(start, SUBLANES, stride=halves), :]
            low = cells % SUBLANES
            high = cells // SUBLANES - step * chunks
            slot = half * groups + group

            def pick(chunk, found):
                rows = pl.ds(pl.multiple_of(chunk * SUBLANES, SUBLANES), SUBLANES)
                hit = high == chunk
                out = []
                for k in range(3):
                    tile = field_ref[k, rows, half * LANES : (half + 1) * LANES]
                    value = jnp.take_along_axis(tile, low, axis=0)
                    out.append(jnp.where(hit, value, found[k]))
                return tuple(out)

            found = tuple(picked_ref[k, slot] for k in range(3))
            found = lax.fori_loop(0, chunks, pick, found, unroll=8)
            for k in range(3):
                picked_ref[k, slot] = found[k]

    @pl.when(step == pl.num_programs(0) - 1)
    def _():
        for half in range(halves):
            for group in range(groups):
                slot = half * groups + group
                where = pl.ds(group * SUBLANES * halves + half, SUBLANES, stride=halves)
                drive_ref[where, :] = (
                    tangent_ref[0, where, :] * picked_ref[0, slot]
                    + tangent_ref[1, where, :] * picked_ref[1, slot]
                    + tangent_ref[2, where, :] * picked_ref[2, slot]
                )


def gather_samples(electric, cells, tangent):
    _, depth, ny, nz = electric.shape
    rows = depth * ny
    steps = 4
    field = electric.reshape(3, rows, nz)
    return pl.pallas_call(
        gather_kernel,
        grid=(steps,),
        out_shape=jax.ShapeDtypeStruct(cells.shape, jnp.float32),
        in_specs=[
            whole_block(cells.shape),
            whole_block(tangent.shape),
            pl.BlockSpec((3, rows // steps, nz), lambda i: (0, i, 0)),
        ],
        out_specs=whole_block(cells.shape),
        scratch_shapes=[
            pltpu.VMEM((3, cells.shape[0] // SUBLANES, SUBLANES, LANES), jnp.float32)
        ],
        compiler_params=params("arbitrary"),
        name="gather_samples",
    )(cells, tangent, field)


def ahead(x, axis):
    extent = x.shape[axis]
    index = lax.broadcasted_iota(jnp.int32, x.shape, axis)
    return jnp.where(index == extent - 1, 0.0, pltpu.roll(x, extent - 1, axis)) - x


def behind(x, axis):
    index = lax.broadcasted_iota(jnp.int32, x.shape, axis)
    return x - jnp.where(index == 0, 0.0, pltpu.roll(x, 1, axis))


def magnetic_kernel(electric_ref, magnetic_ref, above_ref, new_ref, last_ref, next_ref):
    @pl.when(pl.program_id(0) == 0)
    def _():
        next_ref[...] = above_ref[:, 0]

    ex, ey, ez = electric_ref[0, 0], electric_ref[1, 0], electric_ref[2, 0]
    new_ref[0, 0] = magnetic_ref[0, 0] - COURANT * (ahead(ez, 0) - ahead(ey, 1))
    new_y = magnetic_ref[1, 0] - COURANT * (ahead(ex, 1) - (next_ref[1] - ez))
    new_z = magnetic_ref[2, 0] - COURANT * ((next_ref[0] - ey) - ahead(ex, 0))
    new_ref[1, 0] = new_y
    new_ref[2, 0] = new_z
    next_ref[0] = ey
    next_ref[1] = ez

    @pl.when(pl.program_id(0) == 0)
    def _():
        last_ref[0, 0] = new_y
        last_ref[1, 0] = new_z


def magnetic_step(electric, magnetic, above):
    _, depth, ny, nz = electric.shape
    layer = pl.BlockSpec((3, 1, ny, nz), lambda i: (0, depth - 1 - i, 0, 0))
    edge = (2, 1, ny, nz)
    return pl.pallas_call(
        magnetic_kernel,
        grid=(depth,),
        out_shape=[
            jax.ShapeDtypeStruct(magnetic.shape, jnp.float32),
            jax.ShapeDtypeStruct(edge, jnp.float32),
        ],
        in_specs=[layer, layer, whole_block(edge)],
        out_specs=[layer, whole_block(edge)],
        scratch_shapes=[pltpu.VMEM((2, ny, nz), jnp.float32)],
        compiler_params=params("arbitrary"),
        name="magnetic_step",
    )(electric, magnetic, above)


def contract(matrix_ref, vector_ref, finish):
    conductors, segments = vector_ref.shape[0], vector_ref.shape[1]
    tall = 32 if segments % 32 == 0 else SUBLANES
    wide = 4

    def block(i, carry):
        first = i * wide
        for start in range(0, segments, tall):
            rows = slice(start, start + tall)
            sums = [None] * wide
            for d in range(conductors):
                vector = vector_ref[d, rows, :]
                for j in range(wide):
                    term = matrix_ref[first + j, d : d + 1, :] * vector
                    sums[j] = term if d == 0 else sums[j] + term
            for j in range(wide):
                finish(first + j, rows, sums[j])
        return carry

    lax.fori_loop(0, conductors // wide, block, 0)


def line_positions(length_ref, segments):
    lanes = length_ref.shape[1]
    position = lax.broadcasted_iota(jnp.int32, (segments, lanes), 0)
    live = (position < length_ref[...]).astype(jnp.float32)
    last = (position == length_ref[...] - 1).astype(jnp.float32)
    return position, live, last


def set_push(volts_ref, drive_ref, push_ref, position):
    segments = volts_ref.shape[1]

    def one(d, carry):
        volts = volts_ref[d]
        following = jnp.where(
            position == segments - 1, 0.0, pltpu.roll(volts, segments - 1, 0)
        )
        push_ref[d] = following - volts - drive_ref[...]
        return carry

    lax.fori_loop(0, volts_ref.shape[0], one, 0, unroll=4)


def set_slope(amps_ref, slope_ref, position, inflow_ref=None):
    def one(d, carry):
        amps = amps_ref[d]
        edge = 0.0 if inflow_ref is None else inflow_ref[pl.ds(d, 1), :]
        slope_ref[d] = amps - jnp.where(position == 0, edge, pltpu.roll(amps, 1, 0))
        return carry

    lax.fori_loop(0, amps_ref.shape[0], one, 0, unroll=4)


def amps_substep(inductance_ref, push_ref, old_ref, new_ref, live, last, end_ref, slot):
    ends = {}

    def finish(c, rows, total):
        new = live[rows] * (old_ref[c, rows, :] - total)
        new_ref[c, rows, :] = new
        end = jnp.sum(new * last[rows], axis=0, keepdims=True)
        if rows.start > 0:
            end = end + end_ref[slot, pl.ds(c, 1), :]
        end_ref[slot, pl.ds(c, 1), :] = end

    contract(inductance_ref, push_ref, finish)


def volts_substep(capacitance_ref, slope_ref, old_ref, new_ref, live):
    def finish(c, rows, total):
        new_ref[c, rows, :] = live[rows] * (old_ref[c, rows, :] - total)

    contract(capacitance_ref, slope_ref, finish)


def first_lines_kernel(
    drive_ref, volts_ref, amps_ref, inductance_ref, capacitance_ref, length_ref,
    volts_out, amps_out, end_out, work_ref, mid_ref,
):
    position, live, last = line_positions(length_ref, volts_ref.shape[1])
    set_push(volts_ref, drive_ref, work_ref, position)
    amps_substep(inductance_ref, work_ref, amps_ref, mid_ref, live, last, end_out, 0)
    set_slope(mid_ref, work_ref, position)
    volts_substep(capacitance_ref, work_ref, volts_ref, volts_out, live)
    set_push(volts_out, drive_ref, work_ref, position)
    amps_substep(inductance_ref, work_ref, mid_ref, amps_out, live, last, end_out, 1)


def second_lines_kernel(
    drive_ref, volts_ref, amps_ref, inductance_ref, capacitance_ref, length_ref,
    volts_out, amps_out, end_out, total_out, work_ref,
):
    position, live, last = line_positions(length_ref, volts_ref.shape[1])
    set_slope(amps_ref, work_ref, position)
    volts_substep(capacitance_ref, work_ref, volts_ref, volts_out, live)
    set_push(volts_out, drive_ref, work_ref, position)
    amps_substep(inductance_ref, work_ref, amps_ref, amps_out, live, last, end_out, 0)
    total = amps_out[0]
    for c in range(1, amps_out.shape[0]):
        total = total + amps_out[c]
    total_out[...] = total


def feed(end, link):
    picked = []
    for start in range(0, end.shape[0], SUBLANES):
        rows = end[start : start + SUBLANES]
        picked.append(
            jnp.take_along_axis(rows, jnp.broadcast_to(link, rows.shape), axis=1)
        )
    return jnp.concatenate(picked, axis=0)


def apply_symmetric(matrix_ref, vector):
    total = matrix_ref[0] * vector[0:1]
    for d in range(1, vector.shape[0]):
        total = total + matrix_ref[d] * vector[d : d + 1]
    return total


def junction_kernel(
    end_ref, link_ref, inductance_ref, capacitance_ref, total_ref,
    induced_out, amps_shift_out, volts_shift_out,
):
    link = link_ref[...]
    volts0 = apply_symmetric(capacitance_ref, feed(end_ref[0], link))
    fed = apply_symmetric(capacitance_ref, feed(end_ref[1], link))
    amps0 = apply_symmetric(inductance_ref, volts0)
    spread = apply_symmetric(capacitance_ref, amps0)
    volts0 = volts0 - spread + fed
    volts1 = spread
    amps0 = amps0 + apply_symmetric(inductance_ref, volts0 - volts1)
    amps1 = apply_symmetric(inductance_ref, volts1)
    volts_shift_out[0] = volts0
    volts_shift_out[1] = volts1
    amps_shift_out[0] = amps0
    amps_shift_out[1] = amps1
    position = lax.broadcasted_iota(jnp.int32, total_ref.shape, 0)
    conductors = end_ref.shape[1]
    first = jnp.sum(amps0, axis=0, keepdims=True)
    second = jnp.sum(amps1, axis=0, keepdims=True)
    shift = jnp.where(position == 0, first, jnp.where(position == 1, second, 0.0))
    induced_out[...] = (total_ref[...] + shift) * (1.0 / conductors)


def last_lines_kernel(
    end_ref, link_ref, volts_ref, amps_ref, volts_shift_ref, amps_shift_ref,
    capacitance_ref, length_ref, volts_out, amps_out, work_ref, inflow_ref, mid_ref,
):
    position, live, _ = line_positions(length_ref, volts_ref.shape[1])
    inflow_ref[...] = feed(end_ref[0], link_ref[...])

    def shifted(shift_ref, d):
        row = pl.ds(d, 1)
        return jnp.where(
            position == 0, shift_ref[0, row, :],
            jnp.where(position == 1, shift_ref[1, row, :], 0.0),
        )

    def one(d, carry):
        amps_out[d] = amps_ref[d] + shifted(amps_shift_ref, d)
        mid_ref[d] = volts_ref[d] + shifted(volts_shift_ref, d)
        return carry

    lax.fori_loop(0, volts_ref.shape[0], one, 0, unroll=2)
    set_slope(amps_out, work_ref, position, inflow_ref)
    volts_substep(capacitance_ref, work_ref, mid_ref, volts_out, live)


def plain_call(kernel, outs, scratch, name, *operands):
    vmem = pl.BlockSpec(memory_space=pltpu.VMEM)
    return pl.pallas_call(
        kernel,
        out_shape=[jax.ShapeDtypeStruct(shape, jnp.float32) for shape in outs],
        in_specs=[vmem] * len(operands),
        out_specs=[vmem] * len(outs),
        scratch_shapes=[pltpu.VMEM(shape, jnp.float32) for shape in scratch],
        compiler_params=params(),
        name=name,
    )(*operands)


def electric_kernel(
    cell_ref, tangent_ref, induced_ref, electric_ref, magnetic_ref, conductivity_ref,
    below_ref, new_ref, prev_ref, merged_ref, tray_ref,
):
    step = pl.program_id(0)
    ny, nz = new_ref.shape[2], new_ref.shape[3]
    halves = nz // LANES
    trays = cell_ref.shape[0] // halves
    groups = trays // SUBLANES

    @pl.when(step == 0)
    def _():
        prev_ref[...] = below_ref[:, 0]
        for half in range(halves):
            where = pl.ds(half, trays, stride=halves)
            cells = cell_ref[where, :]
            tray_ref[half] = cells
            weights = [tangent_ref[k, where, :] * induced_ref[where, :] for k in range(3)]
            sums = [jnp.zeros_like(w) for w in weights]
            for tray in range(trays):
                same = cells == cells[tray : tray + 1]
                for k in range(3):
                    sums[k] = sums[k] + jnp.where(same, weights[k][tray : tray + 1], 0.0)
            for k in range(3):
                merged_ref[k, half] = sums[k]

    hx, hy, hz = magnetic_ref[0, 0], magnetic_ref[1, 0], magnetic_ref[2, 0]
    new_ref[0, 0] = behind(hz, 0) - behind(hy, 1)
    new_ref[1, 0] = behind(hx, 1) - (hz - prev_ref[1])
    new_ref[2, 0] = (hy - prev_ref[0]) - behind(hx, 0)
    prev_ref[0] = hy
    prev_ref[1] = hz

    for half in range(halves):
        lanes = slice(half * LANES, (half + 1) * LANES)

        def rows_of(chunk, carry):
            first = pl.multiple_of(chunk * SUBLANES, SUBLANES)
            rows = pl.ds(first, SUBLANES)
            here = (
                lax.broadcasted_iota(jnp.int32, (SUBLANES, LANES), 0) + first + step * ny
            )
            code = jnp.full((SUBLANES, LANES), trays, jnp.int32)
            for tray in range(trays):
                code = jnp.where(tray_ref[half, tray : tray + 1, :] == here, tray, code)
            low = code % SUBLANES
            group_of = code // SUBLANES
            sigma = conductivity_ref[0, rows, lanes]
            inverse = 1.0 / (1.0 + sigma)
            keep = (1.0 - sigma) * inverse
            curl = COURANT * inverse
            for k in range(3):
                deposit = jnp.zeros((SUBLANES, LANES), jnp.float32)
                for group in range(groups):
                    part = merged_ref[k, half, group * SUBLANES : (group + 1) * SUBLANES, :]
                    value = jnp.take_along_axis(part, low, axis=0)
                    deposit = jnp.where(group_of == group, value, deposit)
                new_ref[k, 0, rows, lanes] = keep * electric_ref[k, 0, rows, lanes] + curl * (
                    new_ref[k, 0, rows, lanes] - deposit
                )
            return carry

        lax.fori_loop(0, ny // SUBLANES, rows_of, 0, unroll=2)


def electric_step(electric, magnetic_new, conductivity, below, cells, tangent, induced):
    _, depth, ny, nz = electric.shape
    layer = pl.BlockSpec((3, 1, ny, nz), lambda i: (0, i, 0, 0))
    halves = nz // LANES
    trays = cells.shape[0] // halves
    return pl.pallas_call(
        electric_kernel,
        grid=(depth,),
        out_shape=jax.ShapeDtypeStruct(electric.shape, jnp.float32),
        in_specs=[
            whole_block(cells.shape),
            whole_block(tangent.shape),
            whole_block(induced.shape),
            layer,
            layer,
            pl.BlockSpec((1, ny, nz), lambda i: (i, 0, 0)),
            whole_block(below.shape),
        ],
        out_specs=layer,
        scratch_shapes=[
            pltpu.VMEM((2, ny, nz), jnp.float32),
            pltpu.VMEM((3, halves, trays, LANES), jnp.float32),
            pltpu.VMEM((halves, trays, LANES), jnp.int32),
        ],
        compiler_params=params("arbitrary"),
        name="electric_step",
    )(cells, tangent, induced, electric, magnetic_new, conductivity, below)


def local(
    electric,
    magnetic,
    conductivity,
    voltage,
    current,
    inverse_inductance,
    inverse_capacitance,
    tangent,
    sample_cell,
    tube_length,
    junction_link,
):
    conductors, segments, tubes = voltage.shape
    devices = lax.axis_size(AXES)
    own_segments = sample_cell.shape[0]
    cells = sample_cell.reshape(-1, LANES)
    steer = tangent.reshape(3, -1, LANES)
    length = tube_length[None, :]
    link = junction_link[None, :]
    lines = voltage.shape
    end = (conductors, tubes)

    above = passed_along(electric[1:3, 0:1], AXES, -1)
    drive_local = gather_samples(electric, cells, steer)
    drive = lax.all_to_all(
        drive_local.reshape(own_segments, devices, tubes), AXES, split_axis=1, concat_axis=0, tiled=True
    ).reshape(segments, tubes)
    magnetic_new, top = magnetic_step(electric, magnetic, above)
    below = passed_along(top, AXES, 1)

    volts, amps, ends = plain_call(
        first_lines_kernel, [lines, lines, (2,) + end], [lines, lines], "first_lines",
        drive, voltage, current, inverse_inductance, inverse_capacitance, length,
    )
    fed = passed_round(ends, "cable", 1)
    volts, amps, ends, total = plain_call(
        second_lines_kernel, [lines, lines, (1,) + end, (segments, tubes)], [lines],
        "second_lines",
        drive, volts, amps, inverse_inductance, inverse_capacitance, length,
    )
    fed_last = passed_round(ends, "cable", 1)
    induced, amps_shift, volts_shift = plain_call(
        junction_kernel, [(segments, tubes), (2,) + end, (2,) + end], [], "junction",
        fed, link, inverse_inductance, inverse_capacitance, total,
    )
    induced_local = lax.all_to_all(
        induced.reshape(segments, 1, tubes), AXES, split_axis=0, concat_axis=1, tiled=True
    ).reshape(-1, LANES)
    volts, amps = plain_call(
        last_lines_kernel, [lines, lines], [lines, end, lines], "last_lines",
        fed_last, link, volts, amps, volts_shift, amps_shift, inverse_capacitance, length,
    )
    electric_new = electric_step(
        electric, magnetic_new, conductivity, below, cells, steer, induced_local
    )
    return (electric_new, magnetic_new, volts, amps)


def solution(mesh):
    return jax.shard_map(
        local,
        mesh=mesh,
        in_specs=(
            P(None, AXES, None, None),
            P(None, AXES, None, None),
            P(AXES, None, None),
            P(None, None, AXES),
            P(None, None, AXES),
            P(None, None, AXES),
            P(None, None, AXES),
            P(None, AXES, None),
            P(AXES, None),
            P(AXES),
            P(AXES),
        ),
        out_specs=(
            P(None, AXES, None, None),
            P(None, AXES, None, None),
            P(None, None, AXES),
            P(None, None, AXES),
        ),
        check_vma=False,
    )
```

```python
import functools

import jax
import jax.numpy as jnp
from jax import lax
from jax.experimental import pallas as pl
from jax.experimental.pallas import tpu as pltpu
from jax.sharding import PartitionSpec as P

COURANT = 0.5
LANES = 128
SUBLANES = 8
AXES = ("slab", "cable")


def passed_round(value, axis, steps):
    count = lax.axis_size(axis)
    pairs = [(source, (source + steps) % count) for source in range(count)]
    return lax.ppermute(value, axis, pairs)


def params(*semantics):
    if semantics:
        return pltpu.CompilerParams(dimension_semantics=semantics)
    return pltpu.CompilerParams()


def whole_block(shape):
    rank = len(shape)
    return pl.BlockSpec(shape, lambda i: (0,) * rank)


def everyone(mesh_shape):
    slabs, cables = mesh_shape
    count = slabs * cables
    me = lax.axis_index("slab") * cables + lax.axis_index("cable")
    return count, me, lambda peer: (peer // cables, peer % cables)


def greet_all(count, me, place):
    barrier = pltpu.get_barrier_semaphore()

    def greet(k, carry):
        pl.semaphore_signal(
            barrier, inc=1, device_id=place((me + k) % count),
            device_id_type=pl.DeviceIdType.MESH,
        )
        return carry

    lax.fori_loop(1, count, greet, 0)
    return lambda: pl.semaphore_wait(barrier, count - 1)


def row_exchange(count, me, place, send_ref, recv_ref, send_sem, recv_sem):
    def outgoing(k):
        peer = (me + k) % count
        return pltpu.make_async_remote_copy(
            src_ref=send_ref.at[peer], dst_ref=recv_ref.at[me],
            send_sem=send_sem.at[k], recv_sem=recv_sem.at[k],
            device_id=place(peer), device_id_type=pl.DeviceIdType.MESH,
        )

    def incoming(k):
        peer = (me + count - k) % count
        return pltpu.make_async_remote_copy(
            src_ref=send_ref.at[peer], dst_ref=recv_ref.at[peer],
            send_sem=send_sem.at[k], recv_sem=recv_sem.at[k],
            device_id=place(peer), device_id_type=pl.DeviceIdType.MESH,
        )

    def start(k, carry):
        outgoing(k).start()
        return carry

    def finish(k, carry):
        outgoing(k).wait_send()
        incoming(k).wait_recv()
        return carry

    return (
        lambda: lax.fori_loop(1, count, start, 0),
        lambda: lax.fori_loop(1, count, finish, 0),
    )


def edge_copy(count, me, place, by, src, dst, send_sem, recv_sem):
    has_target = (me + by >= 0) & (me + by < count)
    has_source = (me - by >= 0) & (me - by < count)
    target = (me + by + count) % count
    copy = pltpu.make_async_remote_copy(
        src_ref=src, dst_ref=dst, send_sem=send_sem, recv_sem=recv_sem,
        device_id=place(target), device_id_type=pl.DeviceIdType.MESH,
    )

    def start():
        @pl.when(has_target)
        def _():
            copy.start()

    def received():
        @pl.when(has_source)
        def _():
            copy.wait_recv()

        @pl.when(jnp.logical_not(has_source))
        def _():
            dst[...] = jnp.zeros(dst.shape, jnp.float32)

    def sent():
        @pl.when(has_target)
        def _():
            copy.wait_send()

    return start, received, sent


def opening_kernel(
    mesh_shape, cell_ref, tangent_ref, electric_hbm, magnetic_hbm, volts_hbm, amps_hbm,
    inductance_hbm, drive_out, above_out, below_out, pre_out,
    field, top_field, volts_ref, amps_ref, inductance_ref, push_ref, flat_ref,
    send_ref, recv_ref, above_ref, top_ref, below_ref,
    load_sem, send_sem, recv_sem, edge_sem,
):
    depth, ny, nz = field.shape[1:]
    count, me, place = everyone(mesh_shape)
    loads = []
    for i in range(depth):
        loads.append(
            pltpu.make_async_copy(electric_hbm.at[:, i], field.at[:, i], load_sem.at[i])
        )
    extra = [
        (magnetic_hbm.at[pl.ds(1, 2), depth - 1], top_field),
        (volts_hbm, volts_ref),
        (amps_hbm, amps_ref),
        (inductance_hbm, inductance_ref),
    ]
    for i, (src, dst) in enumerate(extra):
        loads.append(pltpu.make_async_copy(src, dst, load_sem.at[depth + i]))
    for load in loads:
        load.start()
    greeted = greet_all(count, me, place)

    loads[0].wait()
    greeted()
    send_above, above_here, above_sent = edge_copy(
        count, me, place, -1, field.at[pl.ds(1, 2), 0], above_ref,
        edge_sem.at[0], edge_sem.at[1],
    )
    send_above()

    halves = nz // LANES
    trays = cell_ref.shape[0] // halves
    groups = trays // SUBLANES
    found = {}
    for layer in range(depth):
        if layer > 0:
            loads[layer].wait()
        for half in range(halves):
            for group in range(groups):
                start = group * SUBLANES * halves + half
                cells = cell_ref[pl.ds(start, SUBLANES, stride=halves), :]
                low = cells & (SUBLANES - 1)
                high = cells // SUBLANES - layer * (ny // SUBLANES)

                def pick(chunk, found):
                    rows = pl.ds(pl.multiple_of(chunk * SUBLANES, SUBLANES), SUBLANES)
                    hit = high == chunk
                    out = []
                    for k in range(3):
                        tile = field[k, layer, rows, half * LANES : (half + 1) * LANES]
                        value = jnp.take_along_axis(tile, low, axis=0)
                        out.append(jnp.where(hit, value, found[k]))
                    return tuple(out)

                empty = (jnp.zeros((SUBLANES, LANES), jnp.float32),) * 3
                found[half, group] = lax.fori_loop(
                    0, ny // SUBLANES, pick, found.get((half, group), empty), unroll=4
                )
    for half in range(halves):
        for group in range(groups):
            where = pl.ds(group * SUBLANES * halves + half, SUBLANES, stride=halves)
            x, y, z = found[half, group]
            flat_ref[where, :] = (
                tangent_ref[0, where, :] * x
                + tangent_ref[1, where, :] * y
                + tangent_ref[2, where, :] * z
            )
    for row in range(count):
        send_ref[row] = flat_ref[row : row + 1, :]
    start_rows, finish_rows = row_exchange(
        count, me, place, send_ref, recv_ref, send_sem, recv_sem
    )
    start_rows()

    loads[depth].wait()
    above_here()
    ex, ey, ez = field[0, depth - 1], field[1, depth - 1], field[2, depth - 1]
    top_ref[0] = top_field[0] - COURANT * (ahead(ex, 1) - (above_ref[1] - ez))
    top_ref[1] = top_field[1] - COURANT * ((above_ref[0] - ey) - ahead(ex, 0))
    send_below, below_here, below_sent = edge_copy(
        count, me, place, 1, top_ref, below_ref, edge_sem.at[2], edge_sem.at[3]
    )
    send_below()

    for load in loads[depth + 1 :]:
        load.wait()
    position = lax.broadcasted_iota(jnp.int32, volts_ref.shape[1:], 0)
    set_push(volts_ref, None, push_ref, position)

    def keep(c, rows, total):
        pre_out[c, rows, :] = amps_ref[c, rows, :] - total

    contract(inductance_ref, push_ref, keep)

    recv_ref[me] = flat_ref[pl.ds(me, 1), :]
    above_out[:, 0] = above_ref[...]
    finish_rows()
    for row in range(count):
        drive_out[row : row + 1, :] = recv_ref[row]
    below_here()
    below_out[:, 0] = below_ref[...]
    above_sent()
    below_sent()


def opening(mesh_shape, cells, steer, electric, magnetic, volts, amps, inductance):
    _, depth, ny, nz = electric.shape
    count = mesh_shape[0] * mesh_shape[1]
    assert cells.shape[0] == count
    vmem = pl.BlockSpec(memory_space=pltpu.VMEM)
    hbm = pl.BlockSpec(memory_space=pl.ANY)
    lines = volts.shape
    row = (count, 1, LANES)
    edge = (2, 1, ny, nz)
    scratch = [
        (3, depth, ny, nz), (2, ny, nz), lines, lines, inductance.shape, lines,
        cells.shape, row, row, edge[:1] + edge[2:], edge[:1] + edge[2:],
        edge[:1] + edge[2:],
    ]
    outs = [(lines[1], lines[2]), edge, edge, lines]
    return pl.pallas_call(
        functools.partial(opening_kernel, mesh_shape),
        out_shape=[jax.ShapeDtypeStruct(shape, jnp.float32) for shape in outs],
        in_specs=[vmem, vmem] + [hbm] * 5,
        out_specs=[vmem] * len(outs),
        scratch_shapes=[pltpu.VMEM(shape, jnp.float32) for shape in scratch]
        + [
            pltpu.SemaphoreType.DMA((depth + 4,)),
            pltpu.SemaphoreType.DMA((count,)),
            pltpu.SemaphoreType.DMA((count,)),
            pltpu.SemaphoreType.DMA((4,)),
        ],
        compiler_params=pltpu.CompilerParams(collective_id=0, has_side_effects=True),
        name="opening",
    )(cells, steer, electric, magnetic, volts, amps, inductance)


def ahead(x, axis):
    extent = x.shape[axis]
    index = lax.broadcasted_iota(jnp.int32, x.shape, axis)
    return jnp.where(index == extent - 1, 0.0, pltpu.roll(x, extent - 1, axis)) - x


def behind(x, axis):
    index = lax.broadcasted_iota(jnp.int32, x.shape, axis)
    return x - jnp.where(index == 0, 0.0, pltpu.roll(x, 1, axis))


def contract(matrix_ref, vector_ref, finish):
    conductors, segments = vector_ref.shape[0], vector_ref.shape[1]
    tall = 32 if segments % 32 == 0 else SUBLANES
    wide = 4

    def block(i, carry):
        first = i * wide
        for start in range(0, segments, tall):
            rows = slice(start, start + tall)
            sums = [None] * wide
            for d in range(conductors):
                vector = vector_ref[d, rows, :]
                for j in range(wide):
                    term = matrix_ref[first + j, d : d + 1, :] * vector
                    sums[j] = term if d == 0 else sums[j] + term
            for j in range(wide):
                finish(first + j, rows, sums[j])
        return carry

    lax.fori_loop(0, conductors // wide, block, 0)


def line_positions(length_ref, segments):
    lanes = length_ref.shape[1]
    position = lax.broadcasted_iota(jnp.int32, (segments, lanes), 0)
    live = (position < length_ref[...]).astype(jnp.float32)
    last = (position == length_ref[...] - 1).astype(jnp.float32)
    return position, live, last


def set_push(volts_ref, drive_ref, push_ref, position):
    segments = volts_ref.shape[1]

    def one(d, carry):
        volts = volts_ref[d]
        following = jnp.where(
            position == segments - 1, 0.0, pltpu.roll(volts, segments - 1, 0)
        )
        push = following - volts
        push_ref[d] = push if drive_ref is None else push - drive_ref[...]
        return carry

    lax.fori_loop(0, volts_ref.shape[0], one, 0, unroll=4)


def set_slope(amps_ref, slope_ref, position, inflow_ref=None):
    def one(d, carry):
        amps = amps_ref[d]
        edge = 0.0 if inflow_ref is None else inflow_ref[pl.ds(d, 1), :]
        slope_ref[d] = amps - jnp.where(position == 0, edge, pltpu.roll(amps, 1, 0))
        return carry

    lax.fori_loop(0, amps_ref.shape[0], one, 0, unroll=4)


def amps_substep(inductance_ref, push_ref, old_ref, new_ref, live, last, end_ref, slot):
    ends = {}

    def finish(c, rows, total):
        new = live[rows] * (old_ref[c, rows, :] - total)
        new_ref[c, rows, :] = new
        end = jnp.sum(new * last[rows], axis=0, keepdims=True)
        if rows.start > 0:
            end = end + end_ref[slot, pl.ds(c, 1), :]
        end_ref[slot, pl.ds(c, 1), :] = end

    contract(inductance_ref, push_ref, finish)


def volts_substep(capacitance_ref, slope_ref, old_ref, new_ref, live):
    def finish(c, rows, total):
        new_ref[c, rows, :] = live[rows] * (old_ref[c, rows, :] - total)

    contract(capacitance_ref, slope_ref, finish)


def first_lines_kernel(
    drive_ref, volts_ref, pre_ref, inductance_ref, capacitance_ref, length_ref,
    volts_out, amps_out, end_out, work_ref, mid_ref, sum_ref,
):
    position, live, last = line_positions(length_ref, volts_ref.shape[1])
    total = inductance_ref[0]
    for d in range(1, inductance_ref.shape[0]):
        total = total + inductance_ref[d]
    sum_ref[...] = total

    def driven(c, carry):
        row = pl.ds(c, 1)
        new = live * (pre_ref[c] + sum_ref[row, :] * drive_ref[...])
        mid_ref[c] = new
        end_out[0, row, :] = jnp.sum(new * last, axis=0, keepdims=True)
        return carry

    lax.fori_loop(0, pre_ref.shape[0], driven, 0, unroll=4)
    set_slope(mid_ref, work_ref, position)
    volts_substep(capacitance_ref, work_ref, volts_ref, volts_out, live)
    set_push(volts_out, drive_ref, work_ref, position)
    amps_substep(inductance_ref, work_ref, mid_ref, amps_out, live, last, end_out, 1)


def second_lines_kernel(
    drive_ref, volts_ref, amps_ref, inductance_ref, capacitance_ref, length_ref,
    volts_out, amps_out, end_out, total_out, work_ref,
):
    position, live, last = line_positions(length_ref, volts_ref.shape[1])
    set_slope(amps_ref, work_ref, position)
    volts_substep(capacitance_ref, work_ref, volts_ref, volts_out, live)
    set_push(volts_out, drive_ref, work_ref, position)
    amps_substep(inductance_ref, work_ref, amps_ref, amps_out, live, last, end_out, 0)
    total = amps_out[0]
    for c in range(1, amps_out.shape[0]):
        total = total + amps_out[c]
    total_out[...] = total


def feed(end, link):
    picked = []
    for start in range(0, end.shape[0], SUBLANES):
        rows = end[start : start + SUBLANES]
        picked.append(
            jnp.take_along_axis(rows, jnp.broadcast_to(link, rows.shape), axis=1)
        )
    return jnp.concatenate(picked, axis=0)


def apply_symmetric(matrix_ref, vector):
    total = matrix_ref[0] * vector[0:1]
    for d in range(1, vector.shape[0]):
        total = total + matrix_ref[d] * vector[d : d + 1]
    return total


def junction_kernel(
    end_ref, link_ref, inductance_ref, capacitance_ref, total_ref,
    induced_out, amps_shift_out, volts_shift_out,
):
    link = link_ref[...]
    volts0 = apply_symmetric(capacitance_ref, feed(end_ref[0], link))
    fed = apply_symmetric(capacitance_ref, feed(end_ref[1], link))
    amps0 = apply_symmetric(inductance_ref, volts0)
    spread = apply_symmetric(capacitance_ref, amps0)
    volts0 = volts0 - spread + fed
    volts1 = spread
    amps0 = amps0 + apply_symmetric(inductance_ref, volts0 - volts1)
    amps1 = apply_symmetric(inductance_ref, volts1)
    volts_shift_out[0] = volts0
    volts_shift_out[1] = volts1
    amps_shift_out[0] = amps0
    amps_shift_out[1] = amps1
    position = lax.broadcasted_iota(jnp.int32, total_ref.shape, 0)
    conductors = end_ref.shape[1]
    first = jnp.sum(amps0, axis=0, keepdims=True)
    second = jnp.sum(amps1, axis=0, keepdims=True)
    shift = jnp.where(position == 0, first, jnp.where(position == 1, second, 0.0))
    induced_out[...] = (total_ref[...] + shift) * (1.0 / conductors)


def last_lines_kernel(
    end_ref, link_ref, volts_ref, amps_ref, volts_shift_ref, amps_shift_ref,
    capacitance_ref, length_ref, volts_out, amps_out, work_ref, inflow_ref, mid_ref,
):
    position, live, _ = line_positions(length_ref, volts_ref.shape[1])
    inflow_ref[...] = feed(end_ref[0], link_ref[...])

    def shifted(shift_ref, d):
        row = pl.ds(d, 1)
        return jnp.where(
            position == 0, shift_ref[0, row, :],
            jnp.where(position == 1, shift_ref[1, row, :], 0.0),
        )

    def one(d, carry):
        amps_out[d] = amps_ref[d] + shifted(amps_shift_ref, d)
        mid_ref[d] = volts_ref[d] + shifted(volts_shift_ref, d)
        return carry

    lax.fori_loop(0, volts_ref.shape[0], one, 0, unroll=2)
    set_slope(amps_out, work_ref, position, inflow_ref)
    volts_substep(capacitance_ref, work_ref, mid_ref, volts_out, live)


def plain_call(kernel, outs, scratch, name, *operands):
    vmem = pl.BlockSpec(memory_space=pltpu.VMEM)
    return pl.pallas_call(
        kernel,
        out_shape=[jax.ShapeDtypeStruct(shape, jnp.float32) for shape in outs],
        in_specs=[vmem] * len(operands),
        out_specs=[vmem] * len(outs),
        scratch_shapes=[pltpu.VMEM(shape, jnp.float32) for shape in scratch],
        compiler_params=params(),
        name=name,
    )(*operands)


def electric_kernel(
    cell_ref, tangent_ref, induced_ref, electric_ref, magnetic_ref, conductivity_ref,
    above_ref, below_ref, new_ref, fresh_ref, prev_ref, held_ref, merged_ref, tray_ref,
):
    turn = pl.program_id(0)
    step = turn - 1
    ny, nz = new_ref.shape[2], new_ref.shape[3]
    halves = nz // LANES
    trays = cell_ref.shape[0] // halves
    groups = trays // SUBLANES

    @pl.when(turn == 0)
    def _():
        prev_ref[...] = below_ref[:, 0]
        held_ref[...] = electric_ref[:, 0]
        for half in range(halves):
            where = pl.ds(half, trays, stride=halves)
            cells = cell_ref[where, :]
            tray_ref[half] = cells
            weights = [tangent_ref[k, where, :] * induced_ref[where, :] for k in range(3)]
            sums = [jnp.zeros_like(w) for w in weights]
            for tray in range(trays):
                same = cells == cells[tray : tray + 1]
                for k in range(3):
                    sums[k] = sums[k] + jnp.where(same, weights[k][tray : tray + 1], 0.0)
            for k in range(3):
                merged_ref[k, half] = sums[k]

    @pl.when(turn > 0)
    def _():
        final = turn == pl.num_programs(0) - 1
        next_y = jnp.where(final, above_ref[0, 0], electric_ref[1, 0])
        next_z = jnp.where(final, above_ref[1, 0], electric_ref[2, 0])
        ex, ey, ez = held_ref[0], held_ref[1], held_ref[2]
        fresh_ref[0, 0] = magnetic_ref[0, 0] - COURANT * (ahead(ez, 0) - ahead(ey, 1))
        fresh_ref[1, 0] = magnetic_ref[1, 0] - COURANT * (ahead(ex, 1) - (next_z - ez))
        fresh_ref[2, 0] = magnetic_ref[2, 0] - COURANT * ((next_y - ey) - ahead(ex, 0))
        hx, hy, hz = fresh_ref[0, 0], fresh_ref[1, 0], fresh_ref[2, 0]
        new_ref[0, 0] = behind(hz, 0) - behind(hy, 1)
        new_ref[1, 0] = behind(hx, 1) - (hz - prev_ref[1])
        new_ref[2, 0] = (hy - prev_ref[0]) - behind(hx, 0)
        prev_ref[0] = hy
        prev_ref[1] = hz

        for half in range(halves):
            lanes = slice(half * LANES, (half + 1) * LANES)

            def rows_of(chunk, carry):
                first = pl.multiple_of(chunk * SUBLANES, SUBLANES)
                rows = pl.ds(first, SUBLANES)
                here = (
                    lax.broadcasted_iota(jnp.int32, (SUBLANES, LANES), 0) + first + step * ny
                )
                code = jnp.full((SUBLANES, LANES), trays, jnp.int32)
                for tray in range(trays):
                    code = jnp.where(tray_ref[half, tray : tray + 1, :] == here, tray, code)
                low = code % SUBLANES
                group_of = code // SUBLANES
                sigma = conductivity_ref[0, rows, lanes]
                inverse = 1.0 / (1.0 + sigma)
                keep = (1.0 - sigma) * inverse
                curl = COURANT * inverse
                for k in range(3):
                    deposit = jnp.zeros((SUBLANES, LANES), jnp.float32)
                    for group in range(groups):
                        part = merged_ref[k, half, group * SUBLANES : (group + 1) * SUBLANES, :]
                        value = jnp.take_along_axis(part, low, axis=0)
                        deposit = jnp.where(group_of == group, value, deposit)
                    new_ref[k, 0, rows, lanes] = keep * held_ref[k, rows, lanes] + curl * (
                        new_ref[k, 0, rows, lanes] - deposit
                    )
                return carry

            lax.fori_loop(0, ny // SUBLANES, rows_of, 0, unroll=2)
        held_ref[...] = electric_ref[:, 0]


def field_step(electric, magnetic, conductivity, above, below, cells, tangent, induced):
    _, depth, ny, nz = electric.shape
    halves = nz // LANES
    trays = cells.shape[0] // halves
    layer = (3, 1, ny, nz)
    leading = pl.BlockSpec(layer, lambda i: (0, jnp.minimum(i, depth - 1), 0, 0))
    trailing = pl.BlockSpec(layer, lambda i: (0, jnp.maximum(i - 1, 0), 0, 0))
    return pl.pallas_call(
        electric_kernel,
        grid=(depth + 1,),
        out_shape=[jax.ShapeDtypeStruct(electric.shape, jnp.float32)] * 2,
        in_specs=[
            whole_block(cells.shape),
            whole_block(tangent.shape),
            whole_block(induced.shape),
            leading,
            trailing,
            pl.BlockSpec((1, ny, nz), lambda i: (jnp.maximum(i - 1, 0), 0, 0)),
            whole_block(above.shape),
            whole_block(below.shape),
        ],
        out_specs=[trailing, trailing],
        scratch_shapes=[
            pltpu.VMEM((2, ny, nz), jnp.float32),
            pltpu.VMEM((3, ny, nz), jnp.float32),
            pltpu.VMEM((3, halves, trays, LANES), jnp.float32),
            pltpu.VMEM((halves, trays, LANES), jnp.int32),
        ],
        compiler_params=params("arbitrary"),
        name="field_step",
    )(cells, tangent, induced, electric, magnetic, conductivity, above, below)


def local(
    mesh_shape,
    electric,
    magnetic,
    conductivity,
    voltage,
    current,
    inverse_inductance,
    inverse_capacitance,
    tangent,
    sample_cell,
    tube_length,
    junction_link,
):
    conductors, segments, tubes = voltage.shape
    cells = sample_cell.reshape(-1, LANES)
    steer = tangent.reshape(3, -1, LANES)
    length = tube_length[None, :]
    link = junction_link[None, :]
    lines = voltage.shape
    end = (conductors, tubes)

    drive, above, below, pre = opening(
        mesh_shape, cells, steer, electric, magnetic, voltage, current, inverse_inductance
    )
    volts, amps, ends = plain_call(
        first_lines_kernel, [lines, lines, (2,) + end], [lines, lines, end], "first_lines",
        drive, voltage, pre, inverse_inductance, inverse_capacitance, length,
    )
    fed = passed_round(ends, "cable", 1)
    volts, amps, ends, total = plain_call(
        second_lines_kernel, [lines, lines, (1,) + end, (segments, tubes)], [lines],
        "second_lines",
        drive, volts, amps, inverse_inductance, inverse_capacitance, length,
    )
    fed_last = passed_round(ends, "cable", 1)
    induced, amps_shift, volts_shift = plain_call(
        junction_kernel, [(segments, tubes), (2,) + end, (2,) + end], [], "junction",
        fed, link, inverse_inductance, inverse_capacitance, total,
    )
    induced_local = lax.all_to_all(
        induced.reshape(segments, 1, tubes), AXES, split_axis=0, concat_axis=1, tiled=True
    ).reshape(-1, LANES)
    volts, amps = plain_call(
        last_lines_kernel, [lines, lines], [lines, end, lines], "last_lines",
        fed_last, link, volts, amps, volts_shift, amps_shift, inverse_capacitance, length,
    )
    electric_new, magnetic_new = field_step(
        electric, magnetic, conductivity, above, below, cells, steer, induced_local
    )
    return (electric_new, magnetic_new, volts, amps)


def solution(mesh):
    mesh_shape = (mesh.shape["slab"], mesh.shape["cable"])
    return jax.shard_map(
        functools.partial(local, mesh_shape),
        mesh=mesh,
        in_specs=(
            P(None, AXES, None, None),
            P(None, AXES, None, None),
            P(AXES, None, None),
            P(None, None, AXES),
            P(None, None, AXES),
            P(None, None, AXES),
            P(None, None, AXES),
            P(None, AXES, None),
            P(AXES, None),
            P(AXES),
            P(AXES),
        ),
        out_specs=(
            P(None, AXES, None, None),
            P(None, AXES, None, None),
            P(None, None, AXES),
            P(None, None, AXES),
        ),
        check_vma=False,
    )
```

```python
import functools

import jax
import jax.numpy as jnp
from jax import lax
from jax.experimental import pallas as pl
from jax.experimental.pallas import tpu as pltpu
from jax.sharding import PartitionSpec as P

COURANT = 0.5
LANES = 128
SUBLANES = 8
AXES = ("slab", "cable")


def params(*semantics):
    if semantics:
        return pltpu.CompilerParams(dimension_semantics=semantics)
    return pltpu.CompilerParams()


def whole_block(shape):
    rank = len(shape)
    return pl.BlockSpec(shape, lambda i: (0,) * rank)


def everyone(mesh_shape):
    slabs, cables = mesh_shape
    count = slabs * cables
    me = lax.axis_index("slab") * cables + lax.axis_index("cable")
    return count, me, lambda peer: (peer // cables, peer % cables)


def greet_all(count, me, place):
    barrier = pltpu.get_barrier_semaphore()

    def greet(k, carry):
        pl.semaphore_signal(
            barrier, inc=1, device_id=place((me + k) % count),
            device_id_type=pl.DeviceIdType.MESH,
        )
        return carry

    lax.fori_loop(1, count, greet, 0)
    return lambda: pl.semaphore_wait(barrier, count - 1)


def row_exchange(count, me, place, send_ref, recv_ref, send_sem, recv_sem):
    def outgoing(k):
        peer = (me + k) % count
        return pltpu.make_async_remote_copy(
            src_ref=send_ref.at[peer], dst_ref=recv_ref.at[me],
            send_sem=send_sem.at[k], recv_sem=recv_sem.at[k],
            device_id=place(peer), device_id_type=pl.DeviceIdType.MESH,
        )

    def incoming(k):
        peer = (me + count - k) % count
        return pltpu.make_async_remote_copy(
            src_ref=send_ref.at[peer], dst_ref=recv_ref.at[peer],
            send_sem=send_sem.at[k], recv_sem=recv_sem.at[k],
            device_id=place(peer), device_id_type=pl.DeviceIdType.MESH,
        )

    def start(k, carry):
        outgoing(k).start()
        return carry

    def finish(k, carry):
        outgoing(k).wait_send()
        incoming(k).wait_recv()
        return carry

    return (
        lambda: lax.fori_loop(1, count, start, 0),
        lambda: lax.fori_loop(1, count, finish, 0),
    )


def edge_copy(count, me, place, by, src, dst, send_sem, recv_sem):
    has_target = (me + by >= 0) & (me + by < count)
    has_source = (me - by >= 0) & (me - by < count)
    target = (me + by + count) % count
    copy = pltpu.make_async_remote_copy(
        src_ref=src, dst_ref=dst, send_sem=send_sem, recv_sem=recv_sem,
        device_id=place(target), device_id_type=pl.DeviceIdType.MESH,
    )

    def start():
        @pl.when(has_target)
        def _():
            copy.start()

    def received():
        @pl.when(has_source)
        def _():
            copy.wait_recv()

        @pl.when(jnp.logical_not(has_source))
        def _():
            dst[...] = jnp.zeros(dst.shape, jnp.float32)

    def sent():
        @pl.when(has_target)
        def _():
            copy.wait_send()

    return start, received, sent


def opening_kernel(
    mesh_shape, cell_ref, tangent_ref, electric_hbm, magnetic_hbm, volts_hbm, amps_hbm,
    inductance_hbm, capacitance_hbm, length_ref, link_ref,
    above_out, below_out, induced_out, volts_out, amps_out,
    field, top_field, volts_ref, amps_ref, inductance_ref, capacitance_ref, work_ref,
    flat_ref, send_ref, recv_ref, send_back_ref, recv_back_ref, above_ref, top_ref,
    below_ref, drive_ref, sum_ref, ends_ref, fed_ref, last_end_ref, last_fed_ref,
    amps_shift_ref, volts_shift_ref, inflow_ref,
    load_sem, send_sem, recv_sem, send_back_sem, recv_back_sem, edge_sem, feed_sem,
):
    depth, ny, nz = field.shape[1:]
    count, me, place = everyone(mesh_shape)
    loads = []
    for i in range(depth):
        loads.append(
            pltpu.make_async_copy(electric_hbm.at[:, i], field.at[:, i], load_sem.at[i])
        )
    extra = [
        (magnetic_hbm.at[pl.ds(1, 2), depth - 1], top_field),
        (volts_hbm, volts_ref),
        (amps_hbm, amps_ref),
        (inductance_hbm, inductance_ref),
        (capacitance_hbm, capacitance_ref),
    ]
    for i, (src, dst) in enumerate(extra):
        loads.append(pltpu.make_async_copy(src, dst, load_sem.at[depth + i]))
    for load in loads:
        load.start()
    greeted = greet_all(count, me, place)

    loads[0].wait()
    greeted()
    send_above, above_here, above_sent = edge_copy(
        count, me, place, -1, field.at[pl.ds(1, 2), 0], above_ref,
        edge_sem.at[0], edge_sem.at[1],
    )
    send_above()

    halves = nz // LANES
    trays = cell_ref.shape[0] // halves
    groups = trays // SUBLANES
    found = {}
    for layer in range(depth):
        if layer > 0:
            loads[layer].wait()
        for half in range(halves):
            for group in range(groups):
                start = group * SUBLANES * halves + half
                cells = cell_ref[pl.ds(start, SUBLANES, stride=halves), :]
                low = cells & (SUBLANES - 1)
                high = cells // SUBLANES - layer * (ny // SUBLANES)

                def pick(chunk, found):
                    rows = pl.ds(pl.multiple_of(chunk * SUBLANES, SUBLANES), SUBLANES)
                    hit = high == chunk
                    out = []
                    for k in range(3):
                        tile = field[k, layer, rows, half * LANES : (half + 1) * LANES]
                        value = jnp.take_along_axis(tile, low, axis=0)
                        out.append(jnp.where(hit, value, found[k]))
                    return tuple(out)

                empty = (jnp.zeros((SUBLANES, LANES), jnp.float32),) * 3
                found[half, group] = lax.fori_loop(
                    0, ny // SUBLANES, pick, found.get((half, group), empty), unroll=4
                )
    for half in range(halves):
        for group in range(groups):
            where = pl.ds(group * SUBLANES * halves + half, SUBLANES, stride=halves)
            x, y, z = found[half, group]
            flat_ref[where, :] = (
                tangent_ref[0, where, :] * x
                + tangent_ref[1, where, :] * y
                + tangent_ref[2, where, :] * z
            )
    for row in range(count):
        send_ref[row] = flat_ref[row : row + 1, :]
    start_rows, finish_rows = row_exchange(
        count, me, place, send_ref, recv_ref, send_sem, recv_sem
    )
    start_rows()

    loads[depth].wait()
    above_here()
    ex, ey, ez = field[0, depth - 1], field[1, depth - 1], field[2, depth - 1]
    top_ref[0] = top_field[0] - COURANT * (ahead(ex, 1) - (above_ref[1] - ez))
    top_ref[1] = top_field[1] - COURANT * ((above_ref[0] - ey) - ahead(ex, 0))
    send_below, below_here, below_sent = edge_copy(
        count, me, place, 1, top_ref, below_ref, edge_sem.at[2], edge_sem.at[3]
    )
    send_below()

    for load in loads[depth + 1 :]:
        load.wait()
    position, live, last = line_positions(length_ref, volts_ref.shape[1])
    conductors = volts_ref.shape[0]
    set_push(volts_ref, None, work_ref, position)

    def keep(c, rows, total):
        amps_ref[c, rows, :] = amps_ref[c, rows, :] - total

    contract(inductance_ref, work_ref, keep)
    total = inductance_ref[0]
    for d in range(1, conductors):
        total = total + inductance_ref[d]
    sum_ref[...] = total

    recv_ref[me] = flat_ref[pl.ds(me, 1), :]
    above_out[:, 0] = above_ref[...]
    finish_rows()
    for row in range(count):
        drive_ref[row : row + 1, :] = recv_ref[row]

    def driven(c, carry):
        row = pl.ds(c, 1)
        new = live * (amps_ref[c] + sum_ref[row, :] * drive_ref[...])
        amps_ref[c] = new
        ends_ref[0, row, :] = jnp.sum(new * last, axis=0, keepdims=True)
        return carry

    lax.fori_loop(0, conductors, driven, 0, unroll=4)
    set_slope(amps_ref, work_ref, position)
    volts_substep(capacitance_ref, work_ref, volts_ref, volts_ref, live)
    set_push(volts_ref, drive_ref, work_ref, position)
    amps_substep(inductance_ref, work_ref, amps_ref, amps_ref, live, last, ends_ref, 1)

    cables = mesh_shape[1]
    fed_device = (
        lax.axis_index("slab"),
        (lax.axis_index("cable") + 1) % cables,
    )
    feeds = [
        pltpu.make_async_remote_copy(
            src_ref=src, dst_ref=dst, send_sem=feed_sem.at[2 * i], recv_sem=feed_sem.at[2 * i + 1],
            device_id=fed_device, device_id_type=pl.DeviceIdType.MESH,
        )
        for i, (src, dst) in enumerate([(ends_ref, fed_ref), (last_end_ref, last_fed_ref)])
    ]
    feeds[0].start()
    set_slope(amps_ref, work_ref, position)
    volts_substep(capacitance_ref, work_ref, volts_ref, volts_ref, live)
    set_push(volts_ref, drive_ref, work_ref, position)
    amps_substep(inductance_ref, work_ref, amps_ref, amps_ref, live, last, last_end_ref, 0)
    feeds[1].start()
    feeds[0].wait()
    junction(
        fed_ref, link_ref, inductance_ref, capacitance_ref, amps_ref, flat_ref,
        amps_shift_ref, volts_shift_ref,
    )
    for row in range(count):
        send_back_ref[row] = flat_ref[row : row + 1, :]
    start_back, finish_back = row_exchange(
        count, me, place, send_back_ref, recv_back_ref, send_back_sem, recv_back_sem
    )
    start_back()
    recv_back_ref[me] = flat_ref[pl.ds(me, 1), :]

    def shifted(shift_ref, d):
        row = pl.ds(d, 1)
        return jnp.where(
            position == 0, shift_ref[0, row, :],
            jnp.where(position == 1, shift_ref[1, row, :], 0.0),
        )

    def settle(d, carry):
        amps_out[d] = amps_ref[d] + shifted(amps_shift_ref, d)
        volts_ref[d] = volts_ref[d] + shifted(volts_shift_ref, d)
        return carry

    lax.fori_loop(0, conductors, settle, 0, unroll=2)
    feeds[1].wait()
    inflow_ref[...] = feed(last_fed_ref[0], link_ref[...])
    set_slope(amps_out, work_ref, position, inflow_ref)
    volts_substep(capacitance_ref, work_ref, volts_ref, volts_out, live)

    below_here()
    below_out[:, 0] = below_ref[...]
    above_sent()
    below_sent()
    finish_back()
    for row in range(count):
        induced_out[row : row + 1, :] = recv_back_ref[row]


def opening(
    mesh_shape, cells, steer, electric, magnetic, volts, amps, inductance, capacitance,
    length, link,
):
    _, depth, ny, nz = electric.shape
    count = mesh_shape[0] * mesh_shape[1]
    conductors, segments, tubes = volts.shape
    assert cells.shape[0] == count and segments == count and tubes == LANES
    vmem = pl.BlockSpec(memory_space=pltpu.VMEM)
    hbm = pl.BlockSpec(memory_space=pl.ANY)
    lines = volts.shape
    matrix = inductance.shape
    row = (count, 1, LANES)
    halo = (2, 1, ny, nz)
    edge = (2, ny, nz)
    end = (conductors, tubes)
    rows = (segments, tubes)
    scratch = [
        (3, depth, ny, nz), edge, lines, lines, matrix, matrix, lines,
        rows, row, row, row, row, edge, edge,
        edge, rows, end, (2,) + end, (2,) + end, (1,) + end, (1,) + end,
        (2,) + end, (2,) + end, end,
    ]
    outs = [halo, halo, rows, lines, lines]
    semaphores = [depth + 5, count, count, count, count, 4, 4]
    return pl.pallas_call(
        functools.partial(opening_kernel, mesh_shape),
        out_shape=[jax.ShapeDtypeStruct(shape, jnp.float32) for shape in outs],
        in_specs=[vmem, vmem] + [hbm] * 6 + [vmem, vmem],
        out_specs=[vmem] * len(outs),
        scratch_shapes=[pltpu.VMEM(shape, jnp.float32) for shape in scratch]
        + [pltpu.SemaphoreType.DMA((number,)) for number in semaphores],
        compiler_params=pltpu.CompilerParams(collective_id=0, has_side_effects=True),
        name="lines_and_exchange",
    )(cells, steer, electric, magnetic, volts, amps, inductance, capacitance, length, link)


def ahead(x, axis):
    extent = x.shape[axis]
    index = lax.broadcasted_iota(jnp.int32, x.shape, axis)
    return jnp.where(index == extent - 1, 0.0, pltpu.roll(x, extent - 1, axis)) - x


def behind(x, axis):
    index = lax.broadcasted_iota(jnp.int32, x.shape, axis)
    return x - jnp.where(index == 0, 0.0, pltpu.roll(x, 1, axis))


def contract(matrix_ref, vector_ref, finish):
    conductors, segments = vector_ref.shape[0], vector_ref.shape[1]
    tall = 32 if segments % 32 == 0 else SUBLANES
    wide = 4

    def block(i, carry):
        first = i * wide
        for start in range(0, segments, tall):
            rows = slice(start, start + tall)
            sums = [None] * wide
            for d in range(conductors):
                vector = vector_ref[d, rows, :]
                for j in range(wide):
                    term = matrix_ref[first + j, d : d + 1, :] * vector
                    sums[j] = term if d == 0 else sums[j] + term
            for j in range(wide):
                finish(first + j, rows, sums[j])
        return carry

    lax.fori_loop(0, conductors // wide, block, 0)


def line_positions(length_ref, segments):
    lanes = length_ref.shape[1]
    position = lax.broadcasted_iota(jnp.int32, (segments, lanes), 0)
    live = (position < length_ref[...]).astype(jnp.float32)
    last = (position == length_ref[...] - 1).astype(jnp.float32)
    return position, live, last


def set_push(volts_ref, drive_ref, push_ref, position):
    segments = volts_ref.shape[1]

    def one(d, carry):
        volts = volts_ref[d]
        following = jnp.where(
            position == segments - 1, 0.0, pltpu.roll(volts, segments - 1, 0)
        )
        push = following - volts
        push_ref[d] = push if drive_ref is None else push - drive_ref[...]
        return carry

    lax.fori_loop(0, volts_ref.shape[0], one, 0, unroll=4)


def set_slope(amps_ref, slope_ref, position, inflow_ref=None):
    def one(d, carry):
        amps = amps_ref[d]
        edge = 0.0 if inflow_ref is None else inflow_ref[pl.ds(d, 1), :]
        slope_ref[d] = amps - jnp.where(position == 0, edge, pltpu.roll(amps, 1, 0))
        return carry

    lax.fori_loop(0, amps_ref.shape[0], one, 0, unroll=4)


def amps_substep(inductance_ref, push_ref, old_ref, new_ref, live, last, end_ref, slot):
    ends = {}

    def finish(c, rows, total):
        new = live[rows] * (old_ref[c, rows, :] - total)
        new_ref[c, rows, :] = new
        end = jnp.sum(new * last[rows], axis=0, keepdims=True)
        if rows.start > 0:
            end = end + end_ref[slot, pl.ds(c, 1), :]
        end_ref[slot, pl.ds(c, 1), :] = end

    contract(inductance_ref, push_ref, finish)


def volts_substep(capacitance_ref, slope_ref, old_ref, new_ref, live):
    def finish(c, rows, total):
        new_ref[c, rows, :] = live[rows] * (old_ref[c, rows, :] - total)

    contract(capacitance_ref, slope_ref, finish)


def feed(end, link):
    picked = []
    for start in range(0, end.shape[0], SUBLANES):
        rows = end[start : start + SUBLANES]
        picked.append(
            jnp.take_along_axis(rows, jnp.broadcast_to(link, rows.shape), axis=1)
        )
    return jnp.concatenate(picked, axis=0)


def apply_symmetric(matrix_ref, vector):
    total = matrix_ref[0] * vector[0:1]
    for d in range(1, vector.shape[0]):
        total = total + matrix_ref[d] * vector[d : d + 1]
    return total


def junction(
    end_ref, link_ref, inductance_ref, capacitance_ref, amps_ref,
    induced_out, amps_shift_out, volts_shift_out,
):
    link = link_ref[...]
    volts0 = apply_symmetric(capacitance_ref, feed(end_ref[0], link))
    fed = apply_symmetric(capacitance_ref, feed(end_ref[1], link))
    amps0 = apply_symmetric(inductance_ref, volts0)
    spread = apply_symmetric(capacitance_ref, amps0)
    volts0 = volts0 - spread + fed
    volts1 = spread
    amps0 = amps0 + apply_symmetric(inductance_ref, volts0 - volts1)
    amps1 = apply_symmetric(inductance_ref, volts1)
    volts_shift_out[0] = volts0
    volts_shift_out[1] = volts1
    amps_shift_out[0] = amps0
    amps_shift_out[1] = amps1
    total = amps_ref[0]
    for c in range(1, amps_ref.shape[0]):
        total = total + amps_ref[c]
    position = lax.broadcasted_iota(jnp.int32, total.shape, 0)
    first = jnp.sum(amps0, axis=0, keepdims=True)
    second = jnp.sum(amps1, axis=0, keepdims=True)
    shift = jnp.where(position == 0, first, jnp.where(position == 1, second, 0.0))
    induced_out[...] = (total + shift) / amps_ref.shape[0]


def electric_kernel(
    cell_ref, tangent_ref, induced_ref, electric_ref, magnetic_ref, conductivity_ref,
    above_ref, below_ref, new_ref, fresh_ref, prev_ref, held_ref, merged_ref, tray_ref,
):
    turn = pl.program_id(0)
    step = turn - 1
    ny, nz = new_ref.shape[2], new_ref.shape[3]
    halves = nz // LANES
    trays = cell_ref.shape[0] // halves
    groups = trays // SUBLANES

    @pl.when(turn == 0)
    def _():
        prev_ref[...] = below_ref[:, 0]
        held_ref[...] = electric_ref[:, 0]
        for half in range(halves):
            where = pl.ds(half, trays, stride=halves)
            cells = cell_ref[where, :]
            tray_ref[half] = cells
            weights = [tangent_ref[k, where, :] * induced_ref[where, :] for k in range(3)]
            sums = [jnp.zeros_like(w) for w in weights]
            for tray in range(trays):
                same = cells == cells[tray : tray + 1]
                for k in range(3):
                    sums[k] = sums[k] + jnp.where(same, weights[k][tray : tray + 1], 0.0)
            for k in range(3):
                merged_ref[k, half] = sums[k]

    @pl.when(turn > 0)
    def _():
        final = turn == pl.num_programs(0) - 1
        next_y = jnp.where(final, above_ref[0, 0], electric_ref[1, 0])
        next_z = jnp.where(final, above_ref[1, 0], electric_ref[2, 0])
        ex, ey, ez = held_ref[0], held_ref[1], held_ref[2]
        fresh_ref[0, 0] = magnetic_ref[0, 0] - COURANT * (ahead(ez, 0) - ahead(ey, 1))
        fresh_ref[1, 0] = magnetic_ref[1, 0] - COURANT * (ahead(ex, 1) - (next_z - ez))
        fresh_ref[2, 0] = magnetic_ref[2, 0] - COURANT * ((next_y - ey) - ahead(ex, 0))
        hx, hy, hz = fresh_ref[0, 0], fresh_ref[1, 0], fresh_ref[2, 0]
        new_ref[0, 0] = behind(hz, 0) - behind(hy, 1)
        new_ref[1, 0] = behind(hx, 1) - (hz - prev_ref[1])
        new_ref[2, 0] = (hy - prev_ref[0]) - behind(hx, 0)
        prev_ref[0] = hy
        prev_ref[1] = hz

        for half in range(halves):
            lanes = slice(half * LANES, (half + 1) * LANES)

            def rows_of(chunk, carry):
                first = pl.multiple_of(chunk * SUBLANES, SUBLANES)
                rows = pl.ds(first, SUBLANES)
                here = (
                    lax.broadcasted_iota(jnp.int32, (SUBLANES, LANES), 0) + first + step * ny
                )
                code = jnp.full((SUBLANES, LANES), trays, jnp.int32)
                for tray in range(trays):
                    code = jnp.where(tray_ref[half, tray : tray + 1, :] == here, tray, code)
                low = code % SUBLANES
                group_of = code // SUBLANES
                sigma = conductivity_ref[0, rows, lanes]
                inverse = 1.0 / (1.0 + sigma)
                keep = (1.0 - sigma) * inverse
                curl = COURANT * inverse
                for k in range(3):
                    deposit = jnp.zeros((SUBLANES, LANES), jnp.float32)
                    for group in range(groups):
                        part = merged_ref[k, half, group * SUBLANES : (group + 1) * SUBLANES, :]
                        value = jnp.take_along_axis(part, low, axis=0)
                        deposit = jnp.where(group_of == group, value, deposit)
                    new_ref[k, 0, rows, lanes] = keep * held_ref[k, rows, lanes] + curl * (
                        new_ref[k, 0, rows, lanes] - deposit
                    )
                return carry

            lax.fori_loop(0, ny // SUBLANES, rows_of, 0, unroll=2)
        held_ref[...] = electric_ref[:, 0]


def field_step(electric, magnetic, conductivity, above, below, cells, tangent, induced):
    _, depth, ny, nz = electric.shape
    halves = nz // LANES
    trays = cells.shape[0] // halves
    layer = (3, 1, ny, nz)
    leading = pl.BlockSpec(layer, lambda i: (0, jnp.minimum(i, depth - 1), 0, 0))
    trailing = pl.BlockSpec(layer, lambda i: (0, jnp.maximum(i - 1, 0), 0, 0))
    return pl.pallas_call(
        electric_kernel,
        grid=(depth + 1,),
        out_shape=[jax.ShapeDtypeStruct(electric.shape, jnp.float32)] * 2,
        in_specs=[
            whole_block(cells.shape),
            whole_block(tangent.shape),
            whole_block(induced.shape),
            leading,
            trailing,
            pl.BlockSpec((1, ny, nz), lambda i: (jnp.maximum(i - 1, 0), 0, 0)),
            whole_block(above.shape),
            whole_block(below.shape),
        ],
        out_specs=[trailing, trailing],
        scratch_shapes=[
            pltpu.VMEM((2, ny, nz), jnp.float32),
            pltpu.VMEM((3, ny, nz), jnp.float32),
            pltpu.VMEM((3, halves, trays, LANES), jnp.float32),
            pltpu.VMEM((halves, trays, LANES), jnp.int32),
        ],
        compiler_params=params("arbitrary"),
        name="field_step",
    )(cells, tangent, induced, electric, magnetic, conductivity, above, below)


def local(
    mesh_shape,
    electric,
    magnetic,
    conductivity,
    voltage,
    current,
    inverse_inductance,
    inverse_capacitance,
    tangent,
    sample_cell,
    tube_length,
    junction_link,
):
    cells = sample_cell.reshape(-1, LANES)
    steer = tangent.reshape(3, -1, LANES)
    above, below, induced, volts, amps = opening(
        mesh_shape, cells, steer, electric, magnetic, voltage, current,
        inverse_inductance, inverse_capacitance, tube_length[None, :], junction_link[None, :],
    )
    electric_new, magnetic_new = field_step(
        electric, magnetic, conductivity, above, below, cells, steer, induced
    )
    return (electric_new, magnetic_new, volts, amps)


def solution(mesh):
    mesh_shape = (mesh.shape["slab"], mesh.shape["cable"])
    return jax.shard_map(
        functools.partial(local, mesh_shape),
        mesh=mesh,
        in_specs=(
            P(None, AXES, None, None),
            P(None, AXES, None, None),
            P(AXES, None, None),
            P(None, None, AXES),
            P(None, None, AXES),
            P(None, None, AXES),
            P(None, None, AXES),
            P(None, AXES, None),
            P(AXES, None),
            P(AXES),
            P(AXES),
        ),
        out_specs=(
            P(None, AXES, None, None),
            P(None, AXES, None, None),
            P(None, None, AXES),
            P(None, None, AXES),
        ),
        check_vma=False,
    )
```

```python
import functools

import jax
import jax.numpy as jnp
from jax import lax
from jax.experimental import pallas as pl
from jax.experimental.pallas import tpu as pltpu
from jax.sharding import PartitionSpec as P

COURANT = 0.5
LANES = 128
SUBLANES = 8
AXES = ("slab", "cable")


def params(*semantics):
    if semantics:
        return pltpu.CompilerParams(dimension_semantics=semantics)
    return pltpu.CompilerParams()


def whole_block(shape):
    rank = len(shape)
    return pl.BlockSpec(shape, lambda i: (0,) * rank)


def everyone(mesh_shape):
    slabs, cables = mesh_shape
    count = slabs * cables
    me = lax.axis_index("slab") * cables + lax.axis_index("cable")
    return count, me, lambda peer: (peer // cables, peer % cables)


def greet_all(count, me, place):
    barrier = pltpu.get_barrier_semaphore()

    def greet(k, carry):
        pl.semaphore_signal(
            barrier, inc=1, device_id=place((me + k) % count),
            device_id_type=pl.DeviceIdType.MESH,
        )
        return carry

    lax.fori_loop(1, count, greet, 0)
    return lambda: pl.semaphore_wait(barrier, count - 1)


def row_exchange(count, me, place, send_ref, recv_ref, send_sem, recv_sem):
    def outgoing(k):
        peer = (me + k) % count
        return pltpu.make_async_remote_copy(
            src_ref=send_ref.at[peer], dst_ref=recv_ref.at[me],
            send_sem=send_sem.at[k], recv_sem=recv_sem.at[k],
            device_id=place(peer), device_id_type=pl.DeviceIdType.MESH,
        )

    def incoming(k):
        peer = (me + count - k) % count
        return pltpu.make_async_remote_copy(
            src_ref=send_ref.at[peer], dst_ref=recv_ref.at[peer],
            send_sem=send_sem.at[k], recv_sem=recv_sem.at[k],
            device_id=place(peer), device_id_type=pl.DeviceIdType.MESH,
        )

    def start(k, carry):
        outgoing(k).start()
        return carry

    def finish(k, carry):
        outgoing(k).wait_send()
        incoming(k).wait_recv()
        return carry

    return (
        lambda: lax.fori_loop(1, count, start, 0),
        lambda: lax.fori_loop(1, count, finish, 0),
    )


def edge_copy(count, me, place, by, src, dst, send_sem, recv_sem):
    has_target = (me + by >= 0) & (me + by < count)
    has_source = (me - by >= 0) & (me - by < count)
    target = (me + by + count) % count
    copy = pltpu.make_async_remote_copy(
        src_ref=src, dst_ref=dst, send_sem=send_sem, recv_sem=recv_sem,
        device_id=place(target), device_id_type=pl.DeviceIdType.MESH,
    )

    def start():
        @pl.when(has_target)
        def _():
            copy.start()

    def received():
        @pl.when(has_source)
        def _():
            copy.wait_recv()

        @pl.when(jnp.logical_not(has_source))
        def _():
            dst[...] = jnp.zeros(dst.shape, jnp.float32)

    def sent():
        @pl.when(has_target)
        def _():
            copy.wait_send()

    return start, received, sent


def opening_kernel(
    mesh_shape, cell_ref, tangent_ref, electric_hbm, magnetic_hbm, volts_hbm, amps_hbm,
    inductance_hbm, capacitance_hbm, length_ref, link_ref,
    above_out, below_out, induced_out, volts_out, amps_out,
    field, top_field, volts_ref, amps_ref, inductance_ref, capacitance_ref, work_ref,
    flat_ref, send_ref, recv_ref, send_back_ref, recv_back_ref, above_ref, top_ref,
    below_ref, drive_ref, sum_ref, ends_ref, fed_ref, last_end_ref, last_fed_ref,
    amps_shift_ref, volts_shift_ref, inflow_ref,
    load_sem, send_sem, recv_sem, send_back_sem, recv_back_sem, edge_sem, feed_sem,
):
    depth, ny, nz = field.shape[1:]
    count, me, place = everyone(mesh_shape)
    loads = []
    for i in range(depth):
        loads.append(
            pltpu.make_async_copy(electric_hbm.at[:, i], field.at[:, i], load_sem.at[i])
        )
    extra = [
        (magnetic_hbm.at[pl.ds(1, 2), depth - 1], top_field),
        (volts_hbm, volts_ref),
        (amps_hbm, amps_ref),
        (inductance_hbm, inductance_ref),
        (capacitance_hbm, capacitance_ref),
    ]
    for i, (src, dst) in enumerate(extra):
        loads.append(pltpu.make_async_copy(src, dst, load_sem.at[depth + i]))
    for load in loads:
        load.start()
    greeted = greet_all(count, me, place)

    loads[0].wait()
    greeted()
    send_above, above_here, above_sent = edge_copy(
        count, me, place, -1, field.at[pl.ds(1, 2), 0], above_ref,
        edge_sem.at[0], edge_sem.at[1],
    )
    send_above()

    halves = nz // LANES
    trays = cell_ref.shape[0] // halves
    groups = trays // SUBLANES
    found = {}
    for layer in range(depth):
        if layer > 0:
            loads[layer].wait()
        for half in range(halves):
            for group in range(groups):
                start = group * SUBLANES * halves + half
                cells = cell_ref[pl.ds(start, SUBLANES, stride=halves), :]
                low = cells & (SUBLANES - 1)
                high = (cells >> 3) - layer * (ny // SUBLANES)

                def pick(chunk, found):
                    rows = pl.ds(pl.multiple_of(chunk * SUBLANES, SUBLANES), SUBLANES)
                    hit = high == chunk
                    out = []
                    for k in range(3):
                        tile = field[k, layer, rows, half * LANES : (half + 1) * LANES]
                        value = jnp.take_along_axis(tile, low, axis=0)
                        out.append(jnp.where(hit, value, found[k]))
                    return tuple(out)

                empty = (jnp.zeros((SUBLANES, LANES), jnp.float32),) * 3
                found[half, group] = lax.fori_loop(
                    0, ny // SUBLANES, pick, found.get((half, group), empty), unroll=4
                )
    for half in range(halves):
        for group in range(groups):
            where = pl.ds(group * SUBLANES * halves + half, SUBLANES, stride=halves)
            x, y, z = found[half, group]
            flat_ref[where, :] = (
                tangent_ref[0, where, :] * x
                + tangent_ref[1, where, :] * y
                + tangent_ref[2, where, :] * z
            )
    for row in range(count):
        send_ref[row] = flat_ref[row : row + 1, :]
    start_rows, finish_rows = row_exchange(
        count, me, place, send_ref, recv_ref, send_sem, recv_sem
    )
    start_rows()

    loads[depth].wait()
    above_here()
    ex, ey, ez = field[0, depth - 1], field[1, depth - 1], field[2, depth - 1]
    top_ref[0] = top_field[0] - COURANT * (ahead(ex, 1) - (above_ref[1] - ez))
    top_ref[1] = top_field[1] - COURANT * ((above_ref[0] - ey) - ahead(ex, 0))
    send_below, below_here, below_sent = edge_copy(
        count, me, place, 1, top_ref, below_ref, edge_sem.at[2], edge_sem.at[3]
    )
    send_below()

    for load in loads[depth + 1 :]:
        load.wait()
    position, live, last = line_positions(length_ref, volts_ref.shape[1])
    conductors = volts_ref.shape[0]
    set_push(volts_ref, None, work_ref, position)

    def keep(c, rows, total):
        amps_ref[c, rows, :] = amps_ref[c, rows, :] - total

    contract(inductance_ref, work_ref, keep)
    total = inductance_ref[0]
    for d in range(1, conductors):
        total = total + inductance_ref[d]
    sum_ref[...] = total

    recv_ref[me] = flat_ref[pl.ds(me, 1), :]
    above_out[:, 0] = above_ref[...]
    finish_rows()
    for row in range(count):
        drive_ref[row : row + 1, :] = recv_ref[row]

    def driven(c, carry):
        row = pl.ds(c, 1)
        new = live * (amps_ref[c] + sum_ref[row, :] * drive_ref[...])
        amps_ref[c] = new
        ends_ref[0, row, :] = jnp.sum(new * last, axis=0, keepdims=True)
        return carry

    lax.fori_loop(0, conductors, driven, 0, unroll=4)
    set_slope(amps_ref, work_ref, position)
    volts_substep(capacitance_ref, work_ref, volts_ref, volts_ref, live)
    set_push(volts_ref, drive_ref, work_ref, position)
    amps_substep(inductance_ref, work_ref, amps_ref, amps_ref, live, last, ends_ref, 1)

    cables = mesh_shape[1]
    fed_device = (
        lax.axis_index("slab"),
        (lax.axis_index("cable") + 1) % cables,
    )
    feeds = [
        pltpu.make_async_remote_copy(
            src_ref=src, dst_ref=dst, send_sem=feed_sem.at[2 * i], recv_sem=feed_sem.at[2 * i + 1],
            device_id=fed_device, device_id_type=pl.DeviceIdType.MESH,
        )
        for i, (src, dst) in enumerate([(ends_ref, fed_ref), (last_end_ref, last_fed_ref)])
    ]
    feeds[0].start()
    set_slope(amps_ref, work_ref, position)
    volts_substep(capacitance_ref, work_ref, volts_ref, volts_ref, live)
    set_push(volts_ref, drive_ref, work_ref, position)
    amps_substep(inductance_ref, work_ref, amps_ref, amps_ref, live, last, last_end_ref, 0)
    feeds[1].start()
    feeds[0].wait()
    junction(
        fed_ref, link_ref, inductance_ref, capacitance_ref, amps_ref, flat_ref,
        amps_shift_ref, volts_shift_ref,
    )
    for row in range(count):
        send_back_ref[row] = flat_ref[row : row + 1, :]
    start_back, finish_back = row_exchange(
        count, me, place, send_back_ref, recv_back_ref, send_back_sem, recv_back_sem
    )
    start_back()
    recv_back_ref[me] = flat_ref[pl.ds(me, 1), :]

    def shifted(shift_ref, d):
        row = pl.ds(d, 1)
        return jnp.where(
            position == 0, shift_ref[0, row, :],
            jnp.where(position == 1, shift_ref[1, row, :], 0.0),
        )

    def settle(d, carry):
        amps_out[d] = amps_ref[d] + shifted(amps_shift_ref, d)
        volts_ref[d] = volts_ref[d] + shifted(volts_shift_ref, d)
        return carry

    lax.fori_loop(0, conductors, settle, 0, unroll=2)
    feeds[1].wait()
    inflow_ref[...] = feed(last_fed_ref[0], link_ref[...])
    set_slope(amps_out, work_ref, position, inflow_ref)
    volts_substep(capacitance_ref, work_ref, volts_ref, volts_out, live)

    below_here()
    below_out[:, 0] = below_ref[...]
    above_sent()
    below_sent()
    finish_back()
    for row in range(count):
        induced_out[row : row + 1, :] = recv_back_ref[row]


def opening(
    mesh_shape, cells, steer, electric, magnetic, volts, amps, inductance, capacitance,
    length, link,
):
    _, depth, ny, nz = electric.shape
    count = mesh_shape[0] * mesh_shape[1]
    conductors, segments, tubes = volts.shape
    assert cells.shape[0] == count and segments == count and tubes == LANES
    vmem = pl.BlockSpec(memory_space=pltpu.VMEM)
    hbm = pl.BlockSpec(memory_space=pl.ANY)
    lines = volts.shape
    matrix = inductance.shape
    row = (count, 1, LANES)
    halo = (2, 1, ny, nz)
    edge = (2, ny, nz)
    end = (conductors, tubes)
    rows = (segments, tubes)
    scratch = [
        (3, depth, ny, nz), edge, lines, lines, matrix, matrix, lines,
        rows, row, row, row, row, edge, edge,
        edge, rows, end, (2,) + end, (2,) + end, (1,) + end, (1,) + end,
        (2,) + end, (2,) + end, end,
    ]
    outs = [halo, halo, rows, lines, lines]
    semaphores = [depth + 5, count, count, count, count, 4, 4]
    return pl.pallas_call(
        functools.partial(opening_kernel, mesh_shape),
        out_shape=[jax.ShapeDtypeStruct(shape, jnp.float32) for shape in outs],
        in_specs=[vmem, vmem] + [hbm] * 6 + [vmem, vmem],
        out_specs=[vmem] * len(outs),
        scratch_shapes=[pltpu.VMEM(shape, jnp.float32) for shape in scratch]
        + [pltpu.SemaphoreType.DMA((number,)) for number in semaphores],
        compiler_params=pltpu.CompilerParams(collective_id=0, has_side_effects=True),
        name="lines_and_exchange",
    )(cells, steer, electric, magnetic, volts, amps, inductance, capacitance, length, link)


def at_edge(rolled, axis, last):
    tile = LANES if axis == 1 else SUBLANES
    extent = rolled.shape[axis]
    cut = extent - tile if last else tile
    first = lax.slice_in_dim(rolled, 0, cut, axis=axis)
    second = lax.slice_in_dim(rolled, cut, extent, axis=axis)
    edge = second if last else first
    index = lax.broadcasted_iota(jnp.int32, edge.shape, axis)
    edge = jnp.where(index == (tile - 1 if last else 0), 0.0, edge)
    return jnp.concatenate([first, edge] if last else [edge, second], axis=axis)


def ahead(x, axis):
    return at_edge(pltpu.roll(x, x.shape[axis] - 1, axis), axis, True) - x


def behind(x, axis):
    return x - at_edge(pltpu.roll(x, 1, axis), axis, False)


def contract(matrix_ref, vector_ref, finish):
    conductors, segments = vector_ref.shape[0], vector_ref.shape[1]
    tall = 32 if segments % 32 == 0 else SUBLANES
    wide = 8

    def block(i, carry):
        first = i * wide
        for start in range(0, segments, tall):
            rows = slice(start, start + tall)
            sums = [None] * wide
            for d in range(conductors):
                vector = vector_ref[d, rows, :]
                for j in range(wide):
                    term = matrix_ref[first + j, d : d + 1, :] * vector
                    sums[j] = term if d == 0 else sums[j] + term
            for j in range(wide):
                finish(first + j, rows, sums[j])
        return carry

    lax.fori_loop(0, conductors // wide, block, 0)


def line_positions(length_ref, segments):
    lanes = length_ref.shape[1]
    position = lax.broadcasted_iota(jnp.int32, (segments, lanes), 0)
    live = (position < length_ref[...]).astype(jnp.float32)
    last = (position == length_ref[...] - 1).astype(jnp.float32)
    return position, live, last


def set_push(volts_ref, drive_ref, push_ref, position):
    segments = volts_ref.shape[1]

    def one(d, carry):
        volts = volts_ref[d]
        following = jnp.where(
            position == segments - 1, 0.0, pltpu.roll(volts, segments - 1, 0)
        )
        push = following - volts
        push_ref[d] = push if drive_ref is None else push - drive_ref[...]
        return carry

    lax.fori_loop(0, volts_ref.shape[0], one, 0, unroll=4)


def set_slope(amps_ref, slope_ref, position, inflow_ref=None):
    def one(d, carry):
        amps = amps_ref[d]
        edge = 0.0 if inflow_ref is None else inflow_ref[pl.ds(d, 1), :]
        slope_ref[d] = amps - jnp.where(position == 0, edge, pltpu.roll(amps, 1, 0))
        return carry

    lax.fori_loop(0, amps_ref.shape[0], one, 0, unroll=4)


def amps_substep(inductance_ref, push_ref, old_ref, new_ref, live, last, end_ref, slot):
    ends = {}

    def finish(c, rows, total):
        new = live[rows] * (old_ref[c, rows, :] - total)
        new_ref[c, rows, :] = new
        end = jnp.sum(new * last[rows], axis=0, keepdims=True)
        if rows.start > 0:
            end = end + end_ref[slot, pl.ds(c, 1), :]
        end_ref[slot, pl.ds(c, 1), :] = end

    contract(inductance_ref, push_ref, finish)


def volts_substep(capacitance_ref, slope_ref, old_ref, new_ref, live):
    def finish(c, rows, total):
        new_ref[c, rows, :] = live[rows] * (old_ref[c, rows, :] - total)

    contract(capacitance_ref, slope_ref, finish)


def feed(end, link):
    picked = []
    for start in range(0, end.shape[0], SUBLANES):
        rows = end[start : start + SUBLANES]
        picked.append(
            jnp.take_along_axis(rows, jnp.broadcast_to(link, rows.shape), axis=1)
        )
    return jnp.concatenate(picked, axis=0)


def apply_symmetric(matrix_ref, vector):
    total = matrix_ref[0] * vector[0:1]
    for d in range(1, vector.shape[0]):
        total = total + matrix_ref[d] * vector[d : d + 1]
    return total


def junction(
    end_ref, link_ref, inductance_ref, capacitance_ref, amps_ref,
    induced_out, amps_shift_out, volts_shift_out,
):
    link = link_ref[...]
    volts0 = apply_symmetric(capacitance_ref, feed(end_ref[0], link))
    fed = apply_symmetric(capacitance_ref, feed(end_ref[1], link))
    amps0 = apply_symmetric(inductance_ref, volts0)
    spread = apply_symmetric(capacitance_ref, amps0)
    volts0 = volts0 - spread + fed
    volts1 = spread
    amps0 = amps0 + apply_symmetric(inductance_ref, volts0 - volts1)
    amps1 = apply_symmetric(inductance_ref, volts1)
    volts_shift_out[0] = volts0
    volts_shift_out[1] = volts1
    amps_shift_out[0] = amps0
    amps_shift_out[1] = amps1
    total = amps_ref[0]
    for c in range(1, amps_ref.shape[0]):
        total = total + amps_ref[c]
    position = lax.broadcasted_iota(jnp.int32, total.shape, 0)
    first = jnp.sum(amps0, axis=0, keepdims=True)
    second = jnp.sum(amps1, axis=0, keepdims=True)
    shift = jnp.where(position == 0, first, jnp.where(position == 1, second, 0.0))
    induced_out[...] = (total + shift) / amps_ref.shape[0]


def electric_kernel(
    cell_ref, tangent_ref, induced_ref, electric_ref, magnetic_ref, conductivity_ref,
    above_ref, below_ref, volts_ref, amps_ref, new_ref, fresh_ref, volts_out, amps_out,
    prev_ref, held_ref, merged_ref, tray_ref,
):
    volts_out[...] = volts_ref[...]
    amps_out[...] = amps_ref[...]
    turn = pl.program_id(0)
    step = turn - 1
    ny, nz = new_ref.shape[2], new_ref.shape[3]
    halves = nz // LANES
    trays = cell_ref.shape[0] // halves
    groups = trays // SUBLANES

    @pl.when(turn == 0)
    def _():
        prev_ref[...] = below_ref[:, 0]
        held_ref[...] = electric_ref[:, 0]
        for half in range(halves):
            where = pl.ds(half, trays, stride=halves)
            cells = cell_ref[where, :]
            tray_ref[half] = cells
            weights = [tangent_ref[k, where, :] * induced_ref[where, :] for k in range(3)]
            sums = [jnp.zeros_like(w) for w in weights]
            for tray in range(trays):
                same = cells == cells[tray : tray + 1]
                for k in range(3):
                    sums[k] = sums[k] + jnp.where(same, weights[k][tray : tray + 1], 0.0)
            for k in range(3):
                merged_ref[k, half] = sums[k]

    @pl.when(turn > 0)
    def _():
        final = turn == pl.num_programs(0) - 1
        next_y = jnp.where(final, above_ref[0, 0], electric_ref[1, 0])
        next_z = jnp.where(final, above_ref[1, 0], electric_ref[2, 0])
        ex, ey, ez = held_ref[0], held_ref[1], held_ref[2]
        fresh_ref[0, 0] = magnetic_ref[0, 0] - COURANT * (ahead(ez, 0) - ahead(ey, 1))
        fresh_ref[1, 0] = magnetic_ref[1, 0] - COURANT * (ahead(ex, 1) - (next_z - ez))
        fresh_ref[2, 0] = magnetic_ref[2, 0] - COURANT * ((next_y - ey) - ahead(ex, 0))
        hx, hy, hz = fresh_ref[0, 0], fresh_ref[1, 0], fresh_ref[2, 0]
        new_ref[0, 0] = behind(hz, 0) - behind(hy, 1)
        new_ref[1, 0] = behind(hx, 1) - (hz - prev_ref[1])
        new_ref[2, 0] = (hy - prev_ref[0]) - behind(hx, 0)
        prev_ref[0] = hy
        prev_ref[1] = hz

        for half in range(halves):
            lanes = slice(half * LANES, (half + 1) * LANES)

            def rows_of(chunk, carry):
                first = pl.multiple_of(chunk * SUBLANES, SUBLANES)
                rows = pl.ds(first, SUBLANES)
                here = (
                    lax.broadcasted_iota(jnp.int32, (SUBLANES, LANES), 0) + first + step * ny
                )
                code = jnp.full((SUBLANES, LANES), trays, jnp.int32)
                for tray in range(trays):
                    code = jnp.where(tray_ref[half, tray : tray + 1, :] == here, tray, code)
                low = code & (SUBLANES - 1)
                group_of = code >> 3
                sigma = conductivity_ref[0, rows, lanes]
                inverse = 1.0 / (1.0 + sigma)
                keep = (1.0 - sigma) * inverse
                curl = COURANT * inverse
                for k in range(3):
                    deposit = jnp.zeros((SUBLANES, LANES), jnp.float32)
                    for group in range(groups):
                        part = merged_ref[k, half, group * SUBLANES : (group + 1) * SUBLANES, :]
                        value = jnp.take_along_axis(part, low, axis=0)
                        deposit = jnp.where(group_of == group, value, deposit)
                    new_ref[k, 0, rows, lanes] = keep * held_ref[k, rows, lanes] + curl * (
                        new_ref[k, 0, rows, lanes] - deposit
                    )
                return carry

            lax.fori_loop(0, ny // SUBLANES, rows_of, 0, unroll=2)
        held_ref[...] = electric_ref[:, 0]


def field_step(electric, magnetic, conductivity, above, below, cells, tangent, induced, volts, amps):
    _, depth, ny, nz = electric.shape
    halves = nz // LANES
    trays = cells.shape[0] // halves
    layer = (3, 1, ny, nz)
    share = pl.cdiv(volts.shape[0], depth)
    line = pl.BlockSpec(
        (share,) + volts.shape[1:], lambda i: (jnp.maximum(i - 1, 0), 0, 0)
    )
    leading = pl.BlockSpec(layer, lambda i: (0, jnp.minimum(i, depth - 1), 0, 0))
    trailing = pl.BlockSpec(layer, lambda i: (0, jnp.maximum(i - 1, 0), 0, 0))
    return pl.pallas_call(
        electric_kernel,
        grid=(depth + 1,),
        out_shape=[jax.ShapeDtypeStruct(electric.shape, jnp.float32)] * 2
        + [jax.ShapeDtypeStruct(volts.shape, jnp.float32)] * 2,
        in_specs=[
            whole_block(cells.shape),
            whole_block(tangent.shape),
            whole_block(induced.shape),
            leading,
            trailing,
            pl.BlockSpec((1, ny, nz), lambda i: (jnp.maximum(i - 1, 0), 0, 0)),
            whole_block(above.shape),
            whole_block(below.shape),
            line,
            line,
        ],
        out_specs=[trailing, trailing, line, line],
        scratch_shapes=[
            pltpu.VMEM((2, ny, nz), jnp.float32),
            pltpu.VMEM((3, ny, nz), jnp.float32),
            pltpu.VMEM((3, halves, trays, LANES), jnp.float32),
            pltpu.VMEM((halves, trays, LANES), jnp.int32),
        ],
        compiler_params=params("arbitrary"),
        name="field_step",
    )(cells, tangent, induced, electric, magnetic, conductivity, above, below, volts, amps)


def local(
    mesh_shape,
    electric,
    magnetic,
    conductivity,
    voltage,
    current,
    inverse_inductance,
    inverse_capacitance,
    tangent,
    sample_cell,
    tube_length,
    junction_link,
):
    cells = sample_cell.reshape(-1, LANES)
    steer = tangent.reshape(3, -1, LANES)
    above, below, induced, volts, amps = opening(
        mesh_shape, cells, steer, electric, magnetic, voltage, current,
        inverse_inductance, inverse_capacitance, tube_length[None, :], junction_link[None, :],
    )
    electric_new, magnetic_new, volts, amps = field_step(
        electric, magnetic, conductivity, above, below, cells, steer, induced, volts, amps
    )
    return (electric_new, magnetic_new, volts, amps)


def solution(mesh):
    mesh_shape = (mesh.shape["slab"], mesh.shape["cable"])
    return jax.shard_map(
        functools.partial(local, mesh_shape),
        mesh=mesh,
        in_specs=(
            P(None, AXES, None, None),
            P(None, AXES, None, None),
            P(AXES, None, None),
            P(None, None, AXES),
            P(None, None, AXES),
            P(None, None, AXES),
            P(None, None, AXES),
            P(None, AXES, None),
            P(AXES, None),
            P(AXES),
            P(AXES),
        ),
        out_specs=(
            P(None, AXES, None, None),
            P(None, AXES, None, None),
            P(None, None, AXES),
            P(None, None, AXES),
        ),
        check_vma=False,
    )
```
